512 devices in a mesh: pair: 64 (over z_lo, x, core), aux: 8 (over y, z_hi).
Axes of the slice: x: 4, y: 4, z: 16 (z_hi: 2, z_lo: 8; z = z_hi * 8 + z_lo), core: 2. Of those that a mesh axis runs over, the one named last changes fastest.
Arguments:
- doubles: bfloat16 [128, 512, 512], P('pair', 'aux'), may hold values from -1.796875 to 1.796875
- singles: bfloat16 [256, 512], replicated, may hold values from -0.8984375 to 0.8984375
- vir_slabs: bfloat16 [4096, 8, 512], P(('aux', 'pair')), may hold values from -0.059814453 to 0.059814453
- occ_slabs: bfloat16 [4096, 256, 512], P(('aux', 'pair')), may hold values from -0.029907227 to 0.029907227
- occ_energy: float32 [256], replicated, may hold values from -2 to -0.5
- vir_energy: float32 [8], replicated, may hold values from 0.1 to 1.5
- pair_list: int32 [128, 2], P('pair'), may hold values from 0 to 255
Outputs:
- new_doubles: float32 [128, 8, 8], P('pair', 'aux')
The draws below stay inside these ranges and needn't reach their ends.
All inputs are finite; a program needn't handle non-finite values.
Results may differ from the reference program's by a relative error of at most 0.0005.
Values may be sent and summed in bfloat16 or wider, within the bound.
No kernel may reach another device: no remote copies, remote signals or barrier semaphores. Data moves between devices by JAX's collectives and lax.ppermute only.
A program may use at most 64 MiB of HBM per device.

```python
import jax
import jax.numpy as jnp
from jax import lax

V = 512
O = 256
NAUX = 4096
NWIN = 8
PAIRS = 128


def set_ends(values, key, least, largest):
    longest = values.shape.index(max(values.shape))
    spots = []
    for shift in (0, 1):
        where = [jax.random.randint(jax.random.fold_in(key, axis), (), 0, length) for axis, length in enumerate(values.shape)]
        where[longest] = (where[longest] + shift) % values.shape[longest]
        spots.append(tuple(where))
    return values.at[spots[0]].set(least).at[spots[1]].set(largest)


def block_scale(rng, dims, shards, least, high):
    def one(axis_at, parts):
        draws = jax.random.uniform(jax.random.fold_in(jax.random.fold_in(rng, 6), axis_at), (parts,), jnp.float32, least / len(shards), high / len(shards))
        return jnp.repeat(jnp.exp(draws), dims[axis_at] // parts).reshape((-1,) + (1,) * (len(dims) - axis_at - 1))

    factor_of = one(*shards[0])
    for cut in shards[1:]:
        factor_of = factor_of * one(*cut)
    return factor_of


def normal_values(rng, dims, spread, limit, cuts=(), held_as=jnp.bfloat16):
    values = spread * jax.random.normal(rng, dims, jnp.float32)
    if cuts:
        values = values * block_scale(rng, dims, cuts, -0.22, 0.18)
    return jnp.clip(values, -limit, limit).astype(held_as)


def setup_inputs(seed: int = 0) -> dict:
    splits = jax.random.split(jax.random.key(seed), 8)
    doubles = normal_values(splits[0], (PAIRS, V, V), 0.3, 1.796875, ((0, 64), (1, 8)))
    singles = normal_values(splits[1], (O, V), 0.15, 0.8984375)
    vir_slabs = normal_values(splits[2], (NAUX, NWIN, V), 0.01, 0.059814453, ((0, 512),))
    occ_slabs = normal_values(splits[3], (NAUX, O, V), 0.005, 0.029907227, ((0, 512),))
    occ_energy = jnp.clip(jax.random.uniform(splits[4], (O,), jnp.float32, -2.0, -0.5), -2.0, -0.5)
    vir_energy = jnp.clip(jax.random.uniform(splits[5], (NWIN,), jnp.float32, 0.1, 1.5), 0.1, 1.5)
    pair_list = set_ends(jax.random.randint(splits[6], (PAIRS, 2), 0, O), jax.random.fold_in(splits[6], 1), 0, O - 1).astype(jnp.int32)
    return {"doubles": doubles, "singles": singles, "vir_slabs": vir_slabs, "occ_slabs": occ_slabs, "occ_energy": occ_energy, "vir_energy": vir_energy, "pair_list": pair_list}


def reference(doubles, singles, vir_slabs, occ_slabs, occ_energy, vir_energy, pair_list):
    first_occ = pair_list[:, 0]
    second_occ = pair_list[:, 1]
    row_first = singles[first_occ].astype(jnp.float32)
    row_second = singles[second_occ].astype(jnp.float32)
    tau_amps = (doubles.astype(jnp.float32) + row_first[:, :, None] * row_second[:, None, :]).astype(jnp.bfloat16)
    tau_wide = tau_amps.astype(jnp.float32)
    dressing_cols = singles[:, :NWIN].astype(jnp.float32)
    block_size = 64 if NAUX % 64 == 0 else NAUX
    block_count = NAUX // block_size
    vir_blocks = vir_slabs.reshape(block_count, block_size, NWIN, V)
    occ_blocks = occ_slabs.reshape(block_count, block_size, O, V)

    def accumulate(running, blocks):
        vir_part, occ_part = blocks
        dressed = (vir_part.astype(jnp.float32) - jnp.einsum('ka,qkc->qac', dressing_cols, occ_part.astype(jnp.float32))).astype(jnp.bfloat16)
        dressed_wide = dressed.astype(jnp.float32)
        half_done = jnp.einsum('qac,pcd->pqad', dressed_wide, tau_wide).astype(jnp.bfloat16)
        running = running + jnp.einsum('pqad,qbd->pab', half_done.astype(jnp.float32), dressed_wide)
        return running, None

    residual, _ = lax.scan(accumulate, jnp.zeros((PAIRS, NWIN, NWIN), jnp.float32), (vir_blocks, occ_blocks))
    pair_energy = occ_energy[first_occ] + occ_energy[second_occ]
    denominator = pair_energy[:, None, None] - vir_energy[None, :, None] - vir_energy[None, None, :]
    return doubles[:, :NWIN, :NWIN].astype(jnp.float32) + residual / denominator
```

```python
import jax
import jax.numpy as jnp
from jax import lax
from jax.experimental import pallas as pl
from jax.experimental.pallas import tpu as pltpu
from jax.sharding import Mesh, PartitionSpec as P

NWIN = 8
GROUP = 256
PAIR = ("zm", "zb", "x", "k")
AUX = ("y", "zh")


def ladder_kernel(slab_ref, tau_ref, out_ref, gram_ref):
    step = pl.program_id(0)
    slabs = slab_ref[...]
    groups = [slabs[s : s + GROUP] for s in range(0, slabs.shape[0], GROUP)]
    pair_count = out_ref.shape[0]
    locals_per = tau_ref.shape[2]

    @pl.when(step == 0)
    def _():
        gram_ref[...] = jnp.zeros_like(gram_ref)

    for pair in range(pair_count):
        core, local = divmod(pair, locals_per)
        tau = tau_ref[core, :, local].reshape(slabs.shape[1], tau_ref.shape[4])
        half = jnp.dot(slabs, tau, preferred_element_type=jnp.float32).astype(jnp.bfloat16)
        total = gram_ref[pair]
        for number, group in enumerate(groups):
            rows = half[number * GROUP : (number + 1) * GROUP]
            total = total + lax.dot_general(
                rows, group, (((1,), (1,)), ((), ())), preferred_element_type=jnp.float32
            )
        gram_ref[pair] = total

    @pl.when(step == pl.num_programs(0) - 1)
    def _():
        row = lax.broadcasted_iota(jnp.int32, (GROUP, GROUP), 0) // NWIN
        col = lax.broadcasted_iota(jnp.int32, (GROUP, GROUP), 1) // NWIN
        same = row == col
        for pair in range(pair_count):
            kept = jnp.where(same, gram_ref[pair], 0.0)
            folded = jnp.sum(kept.reshape(GROUP // NWIN, NWIN, GROUP), axis=0)
            folded = folded[:, :128] + folded[:, 128:]
            shift = 64
            while shift >= NWIN:
                folded = folded + pltpu.roll(folded, shift, 1)
                shift //= 2
            out_ref[pair] = folded


def ladder(slabs, tau, block):
    rows, virt = slabs.shape
    pair_count = tau.shape[0] * tau.shape[2]
    return pl.pallas_call(
        ladder_kernel,
        out_shape=jax.ShapeDtypeStruct((pair_count, NWIN, 128), jnp.float32),
        grid=(rows // block,),
        in_specs=[
            pl.BlockSpec((block, virt), lambda i: (i, 0)),
            pl.BlockSpec(tau.shape, lambda i: (0,) * 5),
        ],
        out_specs=pl.BlockSpec((pair_count, NWIN, 128), lambda i: (0, 0, 0)),
        scratch_shapes=[pltpu.VMEM((pair_count, GROUP, GROUP), jnp.float32)],
        name="ladder",
    )(slabs, tau)


def spread(value, axis):
    copies = jnp.broadcast_to(value[None], (lax.axis_size(axis),) + value.shape)
    return lax.all_to_all(copies, axis, split_axis=0, concat_axis=0, tiled=True)


def after(value, *earlier):
    return lax.optimization_barrier((value,) + earlier)[0]


def body(doubles, singles, vir_slabs, occ_slabs, occ_energy, vir_energy, pair_list):
    local_pairs, chunk, virt = doubles.shape
    occ = singles.shape[0]
    y, zh, core = lax.axis_index("y"), lax.axis_index("zh"), lax.axis_index("k")
    aux = y * 2 + zh
    occ_ids = lax.broadcasted_iota(jnp.int32, (local_pairs, occ), 1)
    match_first = pair_list[:, 0][:, None] == occ_ids
    match_second = pair_list[:, 1][:, None] == occ_ids
    own_cols = lax.dynamic_slice_in_dim(singles, aux * chunk, chunk, 1)
    row_first = jnp.dot(match_first.astype(jnp.bfloat16), own_cols, preferred_element_type=jnp.float32)
    row_second = jnp.dot(match_second.astype(jnp.bfloat16), singles, preferred_element_type=jnp.float32)
    tau = (doubles.astype(jnp.float32) + row_first[:, :, None] * row_second[:, None, :]).astype(jnp.bfloat16)
    dressed = (
        vir_slabs.astype(jnp.float32)
        - jnp.einsum("ka,qkc->qac", singles[:, :NWIN], occ_slabs, preferred_element_type=jnp.float32)
    ).astype(jnp.bfloat16)
    dressed = dressed.reshape(-1, virt)

    other = lax.ppermute(tau, "zh", [(0, 1), (1, 0)])
    dressed = spread(dressed, "zm").reshape(-1, virt)
    dressed_next = lax.ppermute(dressed, "zb", [(0, 1), (1, 0)])
    first = spread(dressed, "x").reshape(-1, virt)
    other = after(other, first)
    both = jnp.where(
        zh == 0, jnp.concatenate([tau, other], axis=1), jnp.concatenate([other, tau], axis=1)
    )
    tau = spread(both, "y")
    dressed_next = after(dressed_next, tau)
    second = spread(dressed_next, "x").reshape(-1, virt)
    tau = spread(tau, "k")
    partial = ladder(jnp.concatenate([first, second], axis=0), tau, 512)[:, :, :NWIN]

    partial = partial.reshape(2, local_pairs, NWIN, NWIN).transpose(0, 2, 1, 3)
    window = doubles[:, :NWIN, :NWIN].astype(jnp.float32).transpose(1, 0, 2)
    mine = (aux == 0) & (lax.broadcasted_iota(jnp.int32, (2, 1, 1, 1), 0) == core)
    window = jnp.where(mine, window[None], 0.0)
    parts = jnp.concatenate([partial, window], axis=-1).reshape(2 * NWIN, local_pairs, 2 * NWIN)
    parts = lax.all_to_all(parts, ("k", "y", "zh"), split_axis=0, concat_axis=0, tiled=True)
    total = jnp.sum(parts, axis=0)
    own_vir = lax.dynamic_slice_in_dim(vir_energy, aux, 1, 0)
    energy_first = jnp.sum(jnp.where(match_first, occ_energy[None, :], 0.0), axis=1)
    energy_second = jnp.sum(jnp.where(match_second, occ_energy[None, :], 0.0), axis=1)
    denominator = (energy_first + energy_second)[:, None] - own_vir - vir_energy[None, :]
    return (total[:, NWIN:] + total[:, :NWIN] / denominator)[:, None, :]


def solution(mesh):
    fine = Mesh(mesh.devices.reshape(4, 2, 4, 2, 4, 2), PAIR + AUX)
    placed = (
        P(PAIR, AUX, None),
        P(),
        P(AUX + PAIR, None, None),
        P(AUX + PAIR, None, None),
        P(),
        P(),
        P(PAIR, None),
    )
    return jax.shard_map(
        body, mesh=fine, in_specs=placed, out_specs=P(PAIR, AUX, None), check_vma=False
    )
```

```python
import jax
import jax.numpy as jnp
from jax import lax
from jax.experimental import pallas as pl
from jax.experimental.pallas import tpu as pltpu
from jax.sharding import Mesh, PartitionSpec as P


NWIN = 8
GROUP = 256
PAIR = ("zm", "zb", "x", "k")
AUX = ("y", "zh")


def ladder_kernel(slab_ref, tau_ref, out_ref, gram_ref):
    step = pl.program_id(0)
    slabs = slab_ref[...]
    groups = [slabs[s : s + GROUP] for s in range(0, slabs.shape[0], GROUP)]
    pair_count = out_ref.shape[0]

    @pl.when(step == 0)
    def _():
        gram_ref[...] = jnp.zeros_like(gram_ref)

    for pair in range(pair_count):
        half = jnp.dot(slabs, tau_ref[pair], preferred_element_type=jnp.float32).astype(jnp.bfloat16)
        total = gram_ref[pair]
        for number, group in enumerate(groups):
            rows = half[number * GROUP : (number + 1) * GROUP]
            total = total + lax.dot_general(
                rows, group, (((1,), (1,)), ((), ())), preferred_element_type=jnp.float32
            )
        gram_ref[pair] = total

    @pl.when(step == pl.num_programs(0) - 1)
    def _():
        row = lax.broadcasted_iota(jnp.int32, (GROUP, GROUP), 0) // NWIN
        col = lax.broadcasted_iota(jnp.int32, (GROUP, GROUP), 1) // NWIN
        same = row == col
        for pair in range(pair_count):
            kept = jnp.where(same, gram_ref[pair], 0.0)
            folded = jnp.sum(kept.reshape(GROUP // NWIN, NWIN, GROUP), axis=0)
            folded = folded[:, :128] + folded[:, 128:]
            shift = 64
            while shift >= NWIN:
                folded = folded + pltpu.roll(folded, shift, 1)
                shift //= 2
            out_ref[pair] = folded


def ladder(slabs, tau, block):
    rows, virt = slabs.shape
    pair_count = tau.shape[0]
    return pl.pallas_call(
        ladder_kernel,
        out_shape=jax.ShapeDtypeStruct((pair_count, NWIN, 128), jnp.float32),
        grid=(rows // block,),
        in_specs=[
            pl.BlockSpec((block, virt), lambda i: (i, 0)),
            pl.BlockSpec(tau.shape, lambda i: (0, 0, 0)),
        ],
        out_specs=pl.BlockSpec((pair_count, NWIN, 128), lambda i: (0, 0, 0)),
        scratch_shapes=[pltpu.VMEM((pair_count, GROUP, GROUP), jnp.float32)],
        cost_estimate=pl.CostEstimate(
            flops=pair_count * rows * virt * (virt + GROUP) * 2,
            bytes_accessed=2 * (rows * virt + pair_count * virt * virt),
            transcendentals=0,
        ),
        name="ladder",
    )(slabs, tau)


def tau_kernel(pairs_ref, aux_ref, doubles_ref, singles_ref, out_ref, cols_ref):
    chunk = doubles_ref.shape[1]
    local_pairs = doubles_ref.shape[0]
    singles = singles_ref[...]
    occ = singles.shape[0]
    ids = lax.broadcasted_iota(jnp.int32, (occ, 128), 0)
    lane = lax.broadcasted_iota(jnp.int32, (occ, 128), 1)
    first = jnp.zeros((occ, 128), jnp.float32)
    for pair in range(local_pairs):
        first = jnp.where((lane == pair) & (ids == pairs_ref[pair, 0]), 1.0, first)
    cols_ref[...] = lax.dot_general(
        singles, first.astype(jnp.bfloat16), (((0,), (0,)), ((), ())), preferred_element_type=jnp.float32
    )
    start = pl.multiple_of(aux_ref[0] * chunk, chunk)
    cols = cols_ref[pl.ds(start, chunk), :]
    ids = lax.broadcasted_iota(jnp.int32, (16, occ), 1)
    row = lax.broadcasted_iota(jnp.int32, (16, occ), 0)
    second = jnp.zeros((16, occ), jnp.float32)
    for pair in range(local_pairs):
        second = jnp.where((row == pair) & (ids == pairs_ref[pair, 1]), 1.0, second)
    rows = jnp.dot(second.astype(jnp.bfloat16), singles, preferred_element_type=jnp.float32)
    for pair in range(local_pairs):
        outer = cols[:, pair : pair + 1] * rows[pair : pair + 1, :]
        out_ref[pair] = (doubles_ref[pair].astype(jnp.float32) + outer).astype(jnp.bfloat16)


def make_tau(doubles, singles, pair_list, aux):
    smem = pl.BlockSpec(memory_space=pltpu.SMEM)
    vmem = pl.BlockSpec(memory_space=pltpu.VMEM)
    return pl.pallas_call(
        tau_kernel,
        out_shape=jax.ShapeDtypeStruct(doubles.shape, jnp.bfloat16),
        in_specs=[smem, smem, vmem, vmem],
        out_specs=vmem,
        scratch_shapes=[pltpu.VMEM((singles.shape[1], 128), jnp.float32)],
        name="tau",
    )(pair_list, aux[None], doubles, singles)


def join_kernel(zh_ref, own_ref, other_ref, out_ref):
    chunk = own_ref.shape[1]
    start = pl.multiple_of(zh_ref[0] * chunk, chunk)
    out_ref[:, pl.ds(start, chunk), :] = own_ref[...]
    out_ref[:, pl.ds(chunk - start, chunk), :] = other_ref[...]


def join(own, other, zh):
    vmem = pl.BlockSpec(memory_space=pltpu.VMEM)
    pairs, chunk, virt = own.shape
    return pl.pallas_call(
        join_kernel,
        out_shape=jax.ShapeDtypeStruct((pairs, 2 * chunk, virt), own.dtype),
        in_specs=[pl.BlockSpec(memory_space=pltpu.SMEM), vmem, vmem],
        out_specs=vmem,
        name="join",
    )(zh[None], own, other)


def assemble_kernel(y_ref, own_ref, below_ref, above_ref, far0_ref, far1_ref, out_ref):
    rows = own_ref.shape[1]

    def place(step):
        return pl.ds(pl.multiple_of(lax.rem(y_ref[0] + step, 4) * rows, rows), rows)

    out_ref[:, place(0), :] = own_ref[...]
    out_ref[:, place(3), :] = below_ref[...]
    out_ref[:, place(1), :] = above_ref[...]
    out_ref[0, place(2), :] = far0_ref[0]
    out_ref[1, place(2), :] = far1_ref[0]


def assemble(y, own, below, above, far0, far1):
    vmem = pl.BlockSpec(memory_space=pltpu.VMEM)
    pairs, rows, virt = own.shape
    return pl.pallas_call(
        assemble_kernel,
        out_shape=jax.ShapeDtypeStruct((pairs, 4 * rows, virt), own.dtype),
        in_specs=[pl.BlockSpec(memory_space=pltpu.SMEM)] + [vmem] * 5,
        out_specs=vmem,
        name="assemble",
    )(y[None], own, below, above, far0, far1)


def spread(value, axis):
    copies = jnp.broadcast_to(value[None], (lax.axis_size(axis),) + value.shape)
    return lax.all_to_all(copies, axis, split_axis=0, concat_axis=0, tiled=True)


SWAP = [(0, 1), (1, 0)]
UP = [(i, (i + 1) % 4) for i in range(4)]
DOWN = [(i, (i + 3) % 4) for i in range(4)]


def step(doubles, singles, vir_slabs, occ_slabs, occ_energy, vir_energy, pair_list):
    local_pairs, _, virt = doubles.shape
    occ = singles.shape[0]
    y, zh, core = lax.axis_index("y"), lax.axis_index("zh"), lax.axis_index("k")
    aux = y * 2 + zh
    tau = make_tau(doubles, singles, pair_list, aux)
    other = lax.ppermute(tau, "zh", SWAP)
    dressed = (
        vir_slabs.astype(jnp.float32)
        - jnp.einsum("ka,qkc->qac", singles[:, :NWIN], occ_slabs, preferred_element_type=jnp.float32)
    ).astype(jnp.bfloat16)
    dressed = dressed.reshape(-1, virt)
    dressed = spread(dressed, "zm").reshape(-1, virt)
    first = spread(dressed, "x").reshape(-1, virt)
    dressed_next = lax.ppermute(dressed, "zb", SWAP)
    both = join(tau, other, zh)
    below = lax.ppermute(both, "y", UP)
    above = lax.ppermute(both, "y", DOWN)
    far0 = lax.ppermute(below[:1], "y", UP)
    far1 = lax.ppermute(above[1:], "y", DOWN)
    tau_own = assemble(y, both, below, above, far0, far1)
    second = spread(dressed_next, "x").reshape(-1, virt)
    tau_other = lax.ppermute(tau_own, "k", SWAP)
    own = ladder(first, tau_own, 512)
    others = ladder(first, tau_other, 512)
    own = own + ladder(second, tau_own, 512)
    others = others + ladder(second, tau_other, 512)

    by_core = jnp.where(core == 0, jnp.stack([own, others]), jnp.stack([others, own]))
    lanes = lax.broadcasted_iota(jnp.int32, (local_pairs, NWIN, 128), 2)
    window = doubles[:, :NWIN, :NWIN].astype(jnp.float32)
    window = jnp.pad(window, ((0, 0), (0, 0), (NWIN, 128 - 2 * NWIN)))
    mine = (aux == 0) & (lax.broadcasted_iota(jnp.int32, (2, 1, 1, 1), 0) == core)
    window = jnp.where(mine, window[None], 0.0)
    parts = jnp.where(lanes < NWIN, by_core, window)
    parts = parts.transpose(0, 2, 1, 3).reshape(2 * NWIN, local_pairs, 128)
    parts = lax.all_to_all(parts, ("k", "y", "zh"), split_axis=0, concat_axis=0, tiled=True)
    total = jnp.sum(parts, axis=0)
    occ_ids = lax.broadcasted_iota(jnp.int32, (local_pairs, occ), 1)
    energies = [
        jnp.sum(jnp.where(pair_list[:, side][:, None] == occ_ids, occ_energy[None, :], 0.0), axis=1)
        for side in (0, 1)
    ]
    own_vir = lax.dynamic_slice_in_dim(vir_energy, aux, 1, 0)
    denominator = (energies[0] + energies[1])[:, None] - own_vir - vir_energy[None, :]
    return (total[:, NWIN : 2 * NWIN] + total[:, :NWIN] / denominator)[:, None, :]


def solution(mesh):
    fine = Mesh(mesh.devices.reshape(4, 2, 4, 2, 4, 2), PAIR + AUX)
    placed = (
        P(PAIR, AUX, None),
        P(),
        P(AUX + PAIR, None, None),
        P(AUX + PAIR, None, None),
        P(),
        P(),
        P(PAIR, None),
    )
    return jax.shard_map(step, mesh=fine, in_specs=placed, out_specs=P(PAIR, AUX, None), check_vma=False)
```

```python
import jax
import jax.numpy as jnp
from jax import lax
from jax.experimental import pallas as pl
from jax.experimental.pallas import tpu as pltpu
from jax.sharding import Mesh, PartitionSpec as P


NWIN = 8
GROUP = 256
BLOCK = 512
PAIR = ("zm", "zb", "x", "k")
AUX = ("y", "zh")
SWAP = [(0, 1), (1, 0)]
UP = [(i, (i + 1) % 4) for i in range(4)]
DOWN = [(i, (i + 3) % 4) for i in range(4)]
SMEM = pl.BlockSpec(memory_space=pltpu.SMEM)
VMEM = pl.BlockSpec(memory_space=pltpu.VMEM)


def start_kernel(
    pairs_ref, place_ref, occ_energy_ref, vir_energy_ref, doubles_ref, singles_ref, vir_ref, occ_ref,
    dressed_ref, tau_ref, denominator_ref, window_ref, cols_ref,
):
    local_pairs, chunk, _ = doubles_ref.shape

    @pl.when(pl.program_id(0) == 0)
    def _():
        window_ref[...] = singles_ref[:, :128].astype(jnp.float32).T[:NWIN].astype(jnp.bfloat16)

    dressed = vir_ref[0].astype(jnp.float32) - jnp.dot(
        window_ref[...], occ_ref[0], preferred_element_type=jnp.float32
    )
    dressed_ref[...] = jnp.broadcast_to(dressed.astype(jnp.bfloat16)[None], dressed_ref.shape)

    @pl.when(pl.program_id(0) == 0)
    def _():
        aux = place_ref[0]
        singles = singles_ref[...]
        occ = singles.shape[0]
        ids = lax.broadcasted_iota(jnp.int32, (occ, 128), 0)
        lane = lax.broadcasted_iota(jnp.int32, (occ, 128), 1)
        first = jnp.zeros((occ, 128), jnp.float32)
        for pair in range(local_pairs):
            first = jnp.where((lane == pair) & (ids == pairs_ref[pair, 0]), 1.0, first)
        cols_ref[...] = lax.dot_general(
            singles, first.astype(jnp.bfloat16), (((0,), (0,)), ((), ())), preferred_element_type=jnp.float32
        )
        cols = cols_ref[pl.ds(pl.multiple_of(aux * chunk, chunk), chunk), :]
        ids = lax.broadcasted_iota(jnp.int32, (16, occ), 1)
        row = lax.broadcasted_iota(jnp.int32, (16, occ), 0)
        second = jnp.zeros((16, occ), jnp.float32)
        for pair in range(local_pairs):
            second = jnp.where((row == pair) & (ids == pairs_ref[pair, 1]), 1.0, second)
        rows = jnp.dot(second.astype(jnp.bfloat16), singles, preferred_element_type=jnp.float32)
        for pair in range(local_pairs):
            outer = cols[:, pair : pair + 1] * rows[pair : pair + 1, :]
            tau_ref[place_ref[1], pair] = (doubles_ref[pair].astype(jnp.float32) + outer).astype(jnp.bfloat16)
        lane = lax.broadcasted_iota(jnp.int32, (1, 128), 1)
        vir = jnp.zeros((1, 128), jnp.float32)
        for b in range(NWIN):
            vir = jnp.where(lane == b, vir_energy_ref[b], vir)
        for pair in range(local_pairs):
            energy = occ_energy_ref[pairs_ref[pair, 0]] + occ_energy_ref[pairs_ref[pair, 1]]
            value = (energy - vir_energy_ref[aux]) - vir
            denominator_ref[pair : pair + 1] = jnp.where(lane < NWIN, value, 1.0)


def start(doubles, singles, vir_slabs, occ_slabs, occ_energy, vir_energy, pair_list, aux, zh):
    local_pairs, chunk, virt = doubles.shape
    slabs, occ, _ = occ_slabs.shape
    return pl.pallas_call(
        start_kernel,
        grid=(slabs,),
        out_shape=(
            jax.ShapeDtypeStruct((4, slabs * NWIN, virt), jnp.bfloat16),
            jax.ShapeDtypeStruct((2, local_pairs, chunk, virt), jnp.bfloat16),
            jax.ShapeDtypeStruct((local_pairs, 128), jnp.float32),
        ),
        in_specs=[
            SMEM, SMEM, SMEM, SMEM,
            pl.BlockSpec(doubles.shape, lambda q: (0, 0, 0)),
            pl.BlockSpec(singles.shape, lambda q: (0, 0)),
            pl.BlockSpec((1, NWIN, virt), lambda q: (q, 0, 0)),
            pl.BlockSpec((1, occ, virt), lambda q: (q, 0, 0)),
        ],
        out_specs=(
            pl.BlockSpec((4, NWIN, virt), lambda q: (0, q, 0)),
            pl.BlockSpec((2, local_pairs, chunk, virt), lambda q: (0, 0, 0, 0)),
            pl.BlockSpec((local_pairs, 128), lambda q: (0, 0)),
        ),
        scratch_shapes=[pltpu.VMEM((NWIN, occ), jnp.bfloat16), pltpu.VMEM((virt, 128), jnp.float32)],
        cost_estimate=pl.CostEstimate(flops=slabs * NWIN * occ * virt * 2, bytes_accessed=3 << 20, transcendentals=0),
        name="start",
    )(pair_list, jnp.stack([aux, zh]), occ_energy, vir_energy, doubles, singles, vir_slabs, occ_slabs)


def gather_tau(y_ref, refs, tau_ref):
    for shift, ref in enumerate(refs):
        halves, pairs, chunk, _ = ref.shape
        base = lax.rem(y_ref[0] + shift, 4) * (halves * chunk)
        for half in range(halves):
            rows = pl.ds(pl.multiple_of(base + half * chunk, chunk), chunk)
            for pair in range(pairs):
                tau_ref[pair, rows, :] = ref[half, pair]


def add_block(slab_ref, tau_ref, gram_ref):
    slabs = slab_ref[...]
    groups = [slabs[s : s + GROUP] for s in range(0, BLOCK, GROUP)]
    for pair in range(tau_ref.shape[0]):
        half = jnp.dot(slabs, tau_ref[pair], preferred_element_type=jnp.float32).astype(jnp.bfloat16)
        total = gram_ref[pair]
        for number, group in enumerate(groups):
            rows = half[number * GROUP : (number + 1) * GROUP]
            total = total + lax.dot_general(
                rows, group, (((1,), (1,)), ((), ())), preferred_element_type=jnp.float32
            )
        gram_ref[pair] = total


def fold(gram):
    row = lax.broadcasted_iota(jnp.int32, (GROUP, GROUP), 0) // NWIN
    col = lax.broadcasted_iota(jnp.int32, (GROUP, GROUP), 1) // NWIN
    kept = jnp.where(row == col, gram, 0.0)
    folded = jnp.sum(kept.reshape(GROUP // NWIN, NWIN, GROUP), axis=0)
    folded = folded[:, :128] + folded[:, 128:]
    shift = 64
    while shift >= NWIN:
        folded = folded + pltpu.roll(folded, shift, 1)
        shift //= 2
    return folded


def ladder_step(y_ref, a_ref, b_ref, tau_refs, tau_ref, gram_ref):
    step = pl.program_id(0)
    half_way = pl.num_programs(0) // 2

    @pl.when(step == 0)
    def _():
        gram_ref[...] = jnp.zeros_like(gram_ref)
        gather_tau(y_ref, tau_refs, tau_ref)

    @pl.when(step < half_way)
    def _():
        add_block(a_ref, tau_ref, gram_ref)

    @pl.when(step >= half_way)
    def _():
        add_block(b_ref, tau_ref, gram_ref)


def first_kernel(place_ref, a_ref, b_ref, t0, t1, t2, t3, out_ref, tau_ref, gram_ref):
    ladder_step(place_ref, a_ref, b_ref, (t0, t1, t2, t3), tau_ref, gram_ref)

    @pl.when(pl.program_id(0) == pl.num_programs(0) - 1)
    def _():
        for pair in range(gram_ref.shape[0]):
            out_ref[pair] = fold(gram_ref[pair])


def second_kernel(
    place_ref, a_ref, b_ref, t0, t1, t2, t3, earlier_ref, doubles_ref, out_ref, tau_ref, gram_ref
):
    ladder_step(place_ref, a_ref, b_ref, (t0, t1, t2, t3), tau_ref, gram_ref)

    @pl.when(pl.program_id(0) == pl.num_programs(0) - 1)
    def _():
        lane = lax.broadcasted_iota(jnp.int32, (NWIN, 128), 1)
        with_doubles = (lane < 2 * NWIN) & (place_ref[1] == 0)
        for pair in range(gram_ref.shape[0]):
            residual = fold(gram_ref[pair]) + earlier_ref[pair]
            doubles = pltpu.roll(doubles_ref[pair].astype(jnp.float32)[:NWIN], NWIN, 1)
            row = jnp.where(lane < NWIN, residual, jnp.where(with_doubles, doubles, 0.0))
            for a in range(NWIN):
                out_ref[a, pair : pair + 1, :] = row[a : a + 1]


def ladder(slabs_a, slabs_b, taus, place, earlier=None, doubles=None):
    rows, virt = slabs_a.shape
    pairs = taus[0].shape[1]
    steps = rows // BLOCK
    whole = pl.BlockSpec(taus[0].shape, lambda i: (0, 0, 0, 0))
    specs = [
        SMEM,
        pl.BlockSpec((BLOCK, virt), lambda i: (jnp.minimum(i, steps - 1), 0)),
        pl.BlockSpec((BLOCK, virt), lambda i: (jnp.maximum(i - steps, 0), 0)),
    ] + [whole] * 4
    operands = [place, slabs_a, slabs_b, *taus]
    if earlier is None:
        kernel, out = first_kernel, (pairs, NWIN, 128)
    else:
        kernel, out = second_kernel, (NWIN, pairs, 128)
        specs += [pl.BlockSpec(earlier.shape, lambda i: (0, 0, 0)), pl.BlockSpec((pairs, 16, 128), lambda i: (0, 0, 0))]
        operands += [earlier, doubles]
    return pl.pallas_call(
        kernel,
        out_shape=jax.ShapeDtypeStruct(out, jnp.float32),
        grid=(2 * steps,),
        in_specs=specs,
        out_specs=pl.BlockSpec(out, lambda i: (0, 0, 0)),
        scratch_shapes=[
            pltpu.VMEM((pairs, virt, virt), jnp.bfloat16),
            pltpu.VMEM((pairs, GROUP, GROUP), jnp.float32),
        ],
        cost_estimate=pl.CostEstimate(
            flops=pairs * rows * virt * (virt + GROUP) * 4,
            bytes_accessed=4 * rows * virt + 2 * pairs * virt * virt,
            transcendentals=0,
        ),
        name="ladder",
    )(*operands)


def last_kernel(parts_ref, denominator_ref, out_ref):
    total = jnp.sum(parts_ref[...], axis=0)
    value = pltpu.roll(total, 128 - NWIN, 1) + total / denominator_ref[...]
    out_ref[...] = value[:, :NWIN]


def last(parts, denominator):
    return pl.pallas_call(
        last_kernel,
        out_shape=jax.ShapeDtypeStruct((parts.shape[1], NWIN), jnp.float32),
        in_specs=[VMEM, VMEM],
        out_specs=VMEM,
        name="last",
    )(parts, denominator)


def exchange(copies, axis):
    return lax.all_to_all(copies, axis, split_axis=0, concat_axis=0, tiled=True)


def spread(value, axis):
    return exchange(jnp.broadcast_to(value[None], (lax.axis_size(axis),) + value.shape), axis)


def body(doubles, singles, vir_slabs, occ_slabs, occ_energy, vir_energy, pair_list):
    virt = doubles.shape[2]
    y, zh = lax.axis_index("y"), lax.axis_index("zh")
    aux = y * 2 + zh
    copies, tau, denominator = start(doubles, singles, vir_slabs, occ_slabs, occ_energy, vir_energy, pair_list, aux, zh)
    dressed = exchange(copies, "zm").reshape(-1, virt)
    own_tau = lax.dynamic_index_in_dim(tau, zh, 0, keepdims=False)
    other = lax.ppermute(own_tau, "zh", SWAP)
    first = spread(dressed, "x").reshape(-1, virt)
    dressed_next = lax.ppermute(dressed, "zb", SWAP)
    tau = lax.dynamic_update_index_in_dim(tau, other, 1 - zh, 0)
    below = lax.ppermute(tau, "y", UP)
    above = lax.ppermute(tau, "y", DOWN)
    second = spread(dressed_next, "x").reshape(-1, virt)
    first_other = lax.ppermute(first, "k", SWAP)
    far = lax.ppermute(below, "y", UP)
    second_other = lax.ppermute(second, "k", SWAP)
    place = jnp.stack([y, aux])
    taus = (tau, above, far, below)
    parts = ladder(first, first_other, taus, place)
    parts = ladder(second, second_other, taus, place, parts, doubles)
    parts = exchange(parts, AUX)
    return last(parts, denominator)[:, None, :]


def solution(mesh):
    fine = Mesh(mesh.devices.reshape(4, 2, 4, 2, 4, 2), PAIR + AUX)
    placed = (
        P(PAIR, AUX, None),
        P(),
        P(AUX + PAIR, None, None),
        P(AUX + PAIR, None, None),
        P(),
        P(),
        P(PAIR, None),
    )
    return jax.shard_map(
        body, mesh=fine, in_specs=placed, out_specs=P(PAIR, AUX, None), check_vma=False
    )
```

```python
import jax
import jax.numpy as jnp
from jax import lax
from jax.experimental import pallas as pl
from jax.experimental.pallas import tpu as pltpu
from jax.sharding import Mesh, PartitionSpec as P


NWIN = 8
GROUP = 256
BLOCK = 512
PAIR = ("zm", "zb", "x", "k")
AUX = ("y", "zh")
SWAP = [(0, 1), (1, 0)]
UP = [(i, (i + 1) % 4) for i in range(4)]
DOWN = [(i, (i + 3) % 4) for i in range(4)]
SMEM = pl.BlockSpec(memory_space=pltpu.SMEM)
VMEM = pl.BlockSpec(memory_space=pltpu.VMEM)


def start_kernel(
    pairs_ref, occ_energy_ref, vir_energy_ref, doubles_ref, singles_ref, vir_ref, occ_ref,
    dressed_ref, own_ref, tau_ref, denominator_ref, cols_ref,
):
    local_pairs, chunk, _ = doubles_ref.shape
    zh = lax.axis_index("zh")
    aux = lax.axis_index("y") * 2 + zh
    singles = singles_ref[...]
    occ = singles.shape[0]
    window = singles[:, :128].astype(jnp.float32).T[:NWIN].astype(jnp.bfloat16)
    for slab in range(occ_ref.shape[0]):
        dressed = vir_ref[slab].astype(jnp.float32) - jnp.dot(
            window, occ_ref[slab], preferred_element_type=jnp.float32
        )
        dressed = dressed.astype(jnp.bfloat16)
        for copy in range(dressed_ref.shape[0]):
            dressed_ref[copy, slab * NWIN : (slab + 1) * NWIN, :] = dressed
    ids = lax.broadcasted_iota(jnp.int32, (occ, 128), 0)
    lane = lax.broadcasted_iota(jnp.int32, (occ, 128), 1)
    first = jnp.zeros((occ, 128), jnp.float32)
    for pair in range(local_pairs):
        first = jnp.where((lane == pair) & (ids == pairs_ref[pair, 0]), 1.0, first)
    cols_ref[...] = lax.dot_general(
        singles, first.astype(jnp.bfloat16), (((0,), (0,)), ((), ())), preferred_element_type=jnp.float32
    )
    cols = cols_ref[pl.ds(pl.multiple_of(aux * chunk, chunk), chunk), :]
    ids = lax.broadcasted_iota(jnp.int32, (16, occ), 1)
    row = lax.broadcasted_iota(jnp.int32, (16, occ), 0)
    second = jnp.zeros((16, occ), jnp.float32)
    for pair in range(local_pairs):
        second = jnp.where((row == pair) & (ids == pairs_ref[pair, 1]), 1.0, second)
    rows = jnp.dot(second.astype(jnp.bfloat16), singles, preferred_element_type=jnp.float32)
    for pair in range(local_pairs):
        outer = cols[:, pair : pair + 1] * rows[pair : pair + 1, :]
        tau = (doubles_ref[pair].astype(jnp.float32) + outer).astype(jnp.bfloat16)
        own_ref[pair] = tau
        tau_ref[zh, pair] = tau
    lane = lax.broadcasted_iota(jnp.int32, (1, 128), 1)
    vir = jnp.zeros((1, 128), jnp.float32)
    for b in range(NWIN):
        vir = jnp.where(lane == b, vir_energy_ref[b], vir)
    for pair in range(local_pairs):
        energy = occ_energy_ref[pairs_ref[pair, 0]] + occ_energy_ref[pairs_ref[pair, 1]]
        value = (energy - vir_energy_ref[aux]) - vir
        denominator_ref[pair : pair + 1] = jnp.where(lane < NWIN, value, 1.0)


def start(doubles, singles, vir_slabs, occ_slabs, occ_energy, vir_energy, pair_list):
    local_pairs, chunk, virt = doubles.shape
    slabs, occ, _ = occ_slabs.shape
    return pl.pallas_call(
        start_kernel,
        out_shape=(
            jax.ShapeDtypeStruct((4, slabs * NWIN, virt), jnp.bfloat16),
            jax.ShapeDtypeStruct((local_pairs, chunk, virt), jnp.bfloat16),
            jax.ShapeDtypeStruct((2, local_pairs, chunk, virt), jnp.bfloat16),
            jax.ShapeDtypeStruct((local_pairs, 128), jnp.float32),
        ),
        in_specs=[SMEM] * 3 + [VMEM] * 4,
        out_specs=(VMEM,) * 4,
        scratch_shapes=[pltpu.VMEM((virt, 128), jnp.float32)],
        cost_estimate=pl.CostEstimate(flops=slabs * NWIN * occ * virt * 2, bytes_accessed=3 << 20, transcendentals=0),
        name="start",
    )(pair_list, occ_energy, vir_energy, doubles, singles, vir_slabs, occ_slabs)


def gather_tau(refs, tau_ref):
    y = lax.axis_index("y")
    for shift, ref in enumerate(refs):
        halves, pairs, chunk, _ = ref.shape
        base = lax.rem(y + shift, 4) * (halves * chunk)
        for half in range(halves):
            rows = pl.ds(pl.multiple_of(base + half * chunk, chunk), chunk)
            for pair in range(pairs):
                tau_ref[pair, rows, :] = ref[half, pair]


def add_block(slab_ref, tau_ref, gram_ref):
    slabs = slab_ref[...]
    groups = [slabs[s : s + GROUP] for s in range(0, BLOCK, GROUP)]
    for pair in range(tau_ref.shape[0]):
        half = jnp.dot(slabs, tau_ref[pair], preferred_element_type=jnp.float32).astype(jnp.bfloat16)
        total = gram_ref[pair]
        for number, group in enumerate(groups):
            rows = half[number * GROUP : (number + 1) * GROUP]
            total = total + lax.dot_general(
                rows, group, (((1,), (1,)), ((), ())), preferred_element_type=jnp.float32
            )
        gram_ref[pair] = total


def fold(gram):
    row = lax.broadcasted_iota(jnp.int32, (GROUP, GROUP), 0) // NWIN
    col = lax.broadcasted_iota(jnp.int32, (GROUP, GROUP), 1) // NWIN
    kept = jnp.where(row == col, gram, 0.0)
    folded = jnp.sum(kept.reshape(GROUP // NWIN, NWIN, GROUP), axis=0)
    folded = folded[:, :128] + folded[:, 128:]
    shift = 64
    while shift >= NWIN:
        folded = folded + pltpu.roll(folded, shift, 1)
        shift //= 2
    return folded


def ladder_step(slab_ref, tau_refs, tau_ref, gram_ref):
    @pl.when(pl.program_id(0) == 0)
    def _():
        gram_ref[...] = jnp.zeros_like(gram_ref)
        gather_tau(tau_refs, tau_ref)

    add_block(slab_ref, tau_ref, gram_ref)


def first_kernel(slab_ref, t0, t1, t2, t3, out_ref, tau_ref, gram_ref):
    ladder_step(slab_ref, (t0, t1, t2, t3), tau_ref, gram_ref)

    @pl.when(pl.program_id(0) == pl.num_programs(0) - 1)
    def _():
        for pair in range(gram_ref.shape[0]):
            out_ref[pair] = fold(gram_ref[pair])


def second_kernel(slab_ref, t0, t1, t2, t3, earlier_ref, doubles_ref, out_ref, tau_ref, gram_ref):
    ladder_step(slab_ref, (t0, t1, t2, t3), tau_ref, gram_ref)

    @pl.when(pl.program_id(0) == pl.num_programs(0) - 1)
    def _():
        lane = lax.broadcasted_iota(jnp.int32, (NWIN, 128), 1)
        holds = (lax.axis_index("y") == 0) & (lax.axis_index("zh") == 0)
        with_doubles = (lane < 2 * NWIN) & holds
        for pair in range(gram_ref.shape[0]):
            residual = fold(gram_ref[pair]) + earlier_ref[pair]
            doubles = pltpu.roll(doubles_ref[pair].astype(jnp.float32)[:NWIN], NWIN, 1)
            row = jnp.where(lane < NWIN, residual, jnp.where(with_doubles, doubles, 0.0))
            for a in range(NWIN):
                out_ref[a, pair : pair + 1, :] = row[a : a + 1]


def ladder(slabs, taus, earlier=None, doubles=None):
    rows, virt = slabs.shape
    pairs = taus[0].shape[1]
    whole = pl.BlockSpec(taus[0].shape, lambda i: (0, 0, 0, 0))
    specs = [pl.BlockSpec((BLOCK, virt), lambda i: (i, 0))] + [whole] * 4
    operands = [slabs, *taus]
    if earlier is None:
        kernel, out = first_kernel, (pairs, NWIN, 128)
    else:
        kernel, out = second_kernel, (NWIN, pairs, 128)
        specs += [pl.BlockSpec(earlier.shape, lambda i: (0, 0, 0)), pl.BlockSpec((pairs, 16, 128), lambda i: (0, 0, 0))]
        operands += [earlier, doubles]
    return pl.pallas_call(
        kernel,
        out_shape=jax.ShapeDtypeStruct(out, jnp.float32),
        grid=(rows // BLOCK,),
        in_specs=specs,
        out_specs=pl.BlockSpec(out, lambda i: (0, 0, 0)),
        scratch_shapes=[
            pltpu.VMEM((pairs, virt, virt), jnp.bfloat16),
            pltpu.VMEM((pairs, GROUP, GROUP), jnp.float32),
        ],
        cost_estimate=pl.CostEstimate(
            flops=pairs * rows * virt * (virt + GROUP) * 2,
            bytes_accessed=2 * rows * virt + 2 * pairs * virt * virt,
            transcendentals=0,
        ),
        name="ladder",
    )(*operands)


def last_kernel(parts_ref, denominator_ref, out_ref):
    total = jnp.sum(parts_ref[...], axis=0)
    value = pltpu.roll(total, 128 - NWIN, 1) + total / denominator_ref[...]
    out_ref[...] = value[:, :NWIN]


def last(parts, denominator):
    return pl.pallas_call(
        last_kernel,
        out_shape=jax.ShapeDtypeStruct((parts.shape[1], NWIN), jnp.float32),
        in_specs=[VMEM, VMEM],
        out_specs=VMEM,
        name="last",
    )(parts, denominator)


def exchange(copies, axis):
    return lax.all_to_all(copies, axis, split_axis=0, concat_axis=0, tiled=True)


def spread(value, axis):
    return exchange(jnp.broadcast_to(value[None], (lax.axis_size(axis),) + value.shape), axis)


def body(doubles, singles, vir_slabs, occ_slabs, occ_energy, vir_energy, pair_list):
    virt = doubles.shape[2]
    zh = lax.axis_index("zh")
    copies, own, tau, denominator = start(doubles, singles, vir_slabs, occ_slabs, occ_energy, vir_energy, pair_list)
    dressed = exchange(copies, "zm").reshape(-1, virt)
    dressed_next = lax.ppermute(dressed, "zb", SWAP)
    other = lax.ppermute(own, "zh", SWAP)
    dressed = spread(jnp.stack([dressed, dressed_next]), "x").reshape(-1, virt)
    tau = lax.dynamic_update_index_in_dim(tau, other, 1 - zh, 0)
    below = lax.ppermute(tau, "y", UP)
    above = lax.ppermute(tau, "y", DOWN)
    far = lax.ppermute(below, "y", UP)
    dressed_other = lax.ppermute(dressed, "k", SWAP)
    taus = (tau, above, far, below)
    parts = ladder(dressed, taus)
    parts = ladder(dressed_other, taus, parts, doubles)
    parts = exchange(parts, AUX)
    return last(parts, denominator)[:, None, :]


def solution(mesh):
    fine = Mesh(mesh.devices.reshape(4, 2, 4, 2, 4, 2), PAIR + AUX)
    placed = (
        P(PAIR, AUX, None),
        P(),
        P(AUX + PAIR, None, None),
        P(AUX + PAIR, None, None),
        P(),
        P(),
        P(PAIR, None),
    )
    return jax.shard_map(
        body, mesh=fine, in_specs=placed, out_specs=P(PAIR, AUX, None), check_vma=False
    )
```

```python
import jax
import jax.numpy as jnp
from jax import lax
from jax.experimental import pallas as pl
from jax.experimental.pallas import tpu as pltpu
from jax.sharding import Mesh, PartitionSpec as P


NWIN = 8
GROUP = 256
BLOCK = 512
PAIR = ("zl", "x", "k")
AUX = ("y", "zh")
SWAP = [(0, 1), (1, 0)]
UP = [(i, (i + 1) % 4) for i in range(4)]
DOWN = [(i, (i + 3) % 4) for i in range(4)]
SMEM = pl.BlockSpec(memory_space=pltpu.SMEM)
VMEM = pl.BlockSpec(memory_space=pltpu.VMEM)


def start_kernel(
    pairs_ref, occ_energy_ref, vir_energy_ref, doubles_ref, singles_ref, vir_ref, occ_ref,
    dressed_ref, low_ref, high_ref, own_ref, tau_ref, denominator_ref, cols_ref,
):
    local_pairs, chunk, _ = doubles_ref.shape
    zh = lax.axis_index("zh")
    aux = lax.axis_index("y") * 2 + zh
    singles = singles_ref[...]
    occ = singles.shape[0]
    window = singles[:, :128].astype(jnp.float32).T[:NWIN].astype(jnp.bfloat16)
    for slab in range(occ_ref.shape[0]):
        dressed = vir_ref[slab].astype(jnp.float32) - jnp.dot(
            window, occ_ref[slab], preferred_element_type=jnp.float32
        )
        dressed_ref[slab * NWIN : (slab + 1) * NWIN, :] = dressed.astype(jnp.bfloat16)
    half = dressed_ref.shape[0] // 2
    low_ref[...] = dressed_ref[:half]
    high_ref[...] = dressed_ref[half:]
    ids = lax.broadcasted_iota(jnp.int32, (occ, 128), 0)
    lane = lax.broadcasted_iota(jnp.int32, (occ, 128), 1)
    first = jnp.zeros((occ, 128), jnp.float32)
    for pair in range(local_pairs):
        first = jnp.where((lane == pair) & (ids == pairs_ref[pair, 0]), 1.0, first)
    cols_ref[...] = lax.dot_general(
        singles, first.astype(jnp.bfloat16), (((0,), (0,)), ((), ())), preferred_element_type=jnp.float32
    )
    cols = cols_ref[pl.ds(pl.multiple_of(aux * chunk, chunk), chunk), :]
    ids = lax.broadcasted_iota(jnp.int32, (16, occ), 1)
    row = lax.broadcasted_iota(jnp.int32, (16, occ), 0)
    second = jnp.zeros((16, occ), jnp.float32)
    for pair in range(local_pairs):
        second = jnp.where((row == pair) & (ids == pairs_ref[pair, 1]), 1.0, second)
    rows = jnp.dot(second.astype(jnp.bfloat16), singles, preferred_element_type=jnp.float32)
    for pair in range(local_pairs):
        outer = cols[:, pair : pair + 1] * rows[pair : pair + 1, :]
        tau = (doubles_ref[pair].astype(jnp.float32) + outer).astype(jnp.bfloat16)
        own_ref[pair] = tau
        tau_ref[zh, pair] = tau
    lane = lax.broadcasted_iota(jnp.int32, (1, 128), 1)
    vir = jnp.zeros((1, 128), jnp.float32)
    for b in range(NWIN):
        vir = jnp.where(lane == b, vir_energy_ref[b], vir)
    for pair in range(local_pairs):
        energy = occ_energy_ref[pairs_ref[pair, 0]] + occ_energy_ref[pairs_ref[pair, 1]]
        value = (energy - vir_energy_ref[aux]) - vir
        denominator_ref[pair : pair + 1] = jnp.where(lane < NWIN, value, 1.0)


def start(doubles, singles, vir_slabs, occ_slabs, occ_energy, vir_energy, pair_list):
    local_pairs, chunk, virt = doubles.shape
    slabs, occ, _ = occ_slabs.shape
    return pl.pallas_call(
        start_kernel,
        out_shape=(
            jax.ShapeDtypeStruct((slabs * NWIN, virt), jnp.bfloat16),
            jax.ShapeDtypeStruct((slabs * NWIN // 2, virt), jnp.bfloat16),
            jax.ShapeDtypeStruct((slabs * NWIN // 2, virt), jnp.bfloat16),
            jax.ShapeDtypeStruct((local_pairs, chunk, virt), jnp.bfloat16),
            jax.ShapeDtypeStruct((2, local_pairs, chunk, virt), jnp.bfloat16),
            jax.ShapeDtypeStruct((local_pairs, 128), jnp.float32),
        ),
        in_specs=[SMEM] * 3 + [VMEM] * 4,
        out_specs=(VMEM,) * 6,
        scratch_shapes=[pltpu.VMEM((virt, 128), jnp.float32)],
        cost_estimate=pl.CostEstimate(flops=slabs * NWIN * occ * virt * 2, bytes_accessed=3 << 20, transcendentals=0),
        name="start",
    )(pair_list, occ_energy, vir_energy, doubles, singles, vir_slabs, occ_slabs)


def gather_tau(refs, tau_ref):
    y = lax.axis_index("y")
    for shift, ref in enumerate(refs):
        halves, pairs, chunk, _ = ref.shape
        base = lax.rem(y + shift, 4) * (halves * chunk)
        for half in range(halves):
            rows = pl.ds(pl.multiple_of(base + half * chunk, chunk), chunk)
            for pair in range(pairs):
                tau_ref[pair, rows, :] = ref[half, pair]


def add_block(slab_ref, tau_ref, gram_ref):
    slabs = slab_ref[...]
    groups = [slabs[s : s + GROUP] for s in range(0, BLOCK, GROUP)]
    for pair in range(tau_ref.shape[0]):
        half = jnp.dot(slabs, tau_ref[pair], preferred_element_type=jnp.float32).astype(jnp.bfloat16)
        total = gram_ref[pair]
        for number, group in enumerate(groups):
            rows = half[number * GROUP : (number + 1) * GROUP]
            total = total + lax.dot_general(
                rows, group, (((1,), (1,)), ((), ())), preferred_element_type=jnp.float32
            )
        gram_ref[pair] = total


def fold(gram):
    row = lax.broadcasted_iota(jnp.int32, (GROUP, GROUP), 0) // NWIN
    col = lax.broadcasted_iota(jnp.int32, (GROUP, GROUP), 1) // NWIN
    kept = jnp.where(row == col, gram, 0.0)
    folded = jnp.sum(kept.reshape(GROUP // NWIN, NWIN, GROUP), axis=0)
    folded = folded[:, :128] + folded[:, 128:]
    shift = 64
    while shift >= NWIN:
        folded = folded + pltpu.roll(folded, shift, 1)
        shift //= 2
    return folded


def ladder_step(slab_ref, tau_refs, tau_ref, gram_ref):
    @pl.when(pl.program_id(0) == 0)
    def _():
        gram_ref[...] = jnp.zeros_like(gram_ref)
        gather_tau(tau_refs, tau_ref)

    add_block(slab_ref, tau_ref, gram_ref)


def first_kernel(slab_ref, t0, t1, t2, t3, out_ref, tau_ref, gram_ref):
    ladder_step(slab_ref, (t0, t1, t2, t3), tau_ref, gram_ref)

    @pl.when(pl.program_id(0) == pl.num_programs(0) - 1)
    def _():
        for pair in range(gram_ref.shape[0]):
            out_ref[pair] = fold(gram_ref[pair])


def second_kernel(slab_ref, t0, t1, t2, t3, earlier_ref, doubles_ref, out_ref, tau_ref, gram_ref):
    ladder_step(slab_ref, (t0, t1, t2, t3), tau_ref, gram_ref)

    @pl.when(pl.program_id(0) == pl.num_programs(0) - 1)
    def _():
        lane = lax.broadcasted_iota(jnp.int32, (NWIN, 128), 1)
        holds = (lax.axis_index("y") == 0) & (lax.axis_index("zh") == 0)
        with_doubles = (lane < 2 * NWIN) & holds
        for pair in range(gram_ref.shape[0]):
            residual = fold(gram_ref[pair]) + earlier_ref[pair]
            doubles = pltpu.roll(doubles_ref[pair].astype(jnp.float32)[:NWIN], NWIN, 1)
            row = jnp.where(lane < NWIN, residual, jnp.where(with_doubles, doubles, 0.0))
            for a in range(NWIN):
                out_ref[a, pair : pair + 1, :] = row[a : a + 1]


def ladder(slabs, taus, earlier=None, doubles=None):
    rows, virt = slabs.shape
    pairs = taus[0].shape[1]
    whole = pl.BlockSpec(taus[0].shape, lambda i: (0, 0, 0, 0))
    specs = [pl.BlockSpec((BLOCK, virt), lambda i: (i, 0))] + [whole] * 4
    operands = [slabs, *taus]
    if earlier is None:
        kernel, out = first_kernel, (pairs, NWIN, 128)
    else:
        kernel, out = second_kernel, (NWIN, pairs, 128)
        specs += [pl.BlockSpec(earlier.shape, lambda i: (0, 0, 0)), pl.BlockSpec((pairs, 16, 128), lambda i: (0, 0, 0))]
        operands += [earlier, doubles]
    return pl.pallas_call(
        kernel,
        out_shape=jax.ShapeDtypeStruct(out, jnp.float32),
        grid=(rows // BLOCK,),
        in_specs=specs,
        out_specs=pl.BlockSpec(out, lambda i: (0, 0, 0)),
        scratch_shapes=[
            pltpu.VMEM((pairs, virt, virt), jnp.bfloat16),
            pltpu.VMEM((pairs, GROUP, GROUP), jnp.float32),
        ],
        cost_estimate=pl.CostEstimate(
            flops=pairs * rows * virt * (virt + GROUP) * 2,
            bytes_accessed=2 * rows * virt + 2 * pairs * virt * virt,
            transcendentals=0,
        ),
        compiler_params=pltpu.CompilerParams(vmem_limit_bytes=16 << 20),
        name="ladder",
    )(*operands)


def last_kernel(parts_ref, denominator_ref, out_ref):
    total = jnp.sum(parts_ref[...], axis=0)
    value = pltpu.roll(total, 128 - NWIN, 1) + total / denominator_ref[...]
    out_ref[...] = value[:, :NWIN]


def last(parts, denominator):
    return pl.pallas_call(
        last_kernel,
        out_shape=jax.ShapeDtypeStruct((parts.shape[1], NWIN), jnp.float32),
        in_specs=[VMEM, VMEM],
        out_specs=VMEM,
        name="last",
    )(parts, denominator)


def exchange(copies, axis):
    return lax.all_to_all(copies, axis, split_axis=0, concat_axis=0, tiled=True)


def shift_z(value, step):
    moves = []
    for z in range(16):
        to = (z + step) % 16
        moves.append((z % 8 * 2 + z // 8, to % 8 * 2 + to // 8))
    return lax.ppermute(value, ("zl", "zh"), moves)


def spread(value, axis):
    return exchange(jnp.broadcast_to(value[None], (lax.axis_size(axis),) + value.shape), axis)


def body(doubles, singles, vir_slabs, occ_slabs, occ_energy, vir_energy, pair_list):
    virt = doubles.shape[2]
    zh = lax.axis_index("zh")
    dressed, low, high, own, tau, denominator = start(
        doubles, singles, vir_slabs, occ_slabs, occ_energy, vir_energy, pair_list
    )
    below_4 = shift_z(low, 4)
    above_4 = shift_z(high, -4)
    below_2 = shift_z(dressed, 2)
    above_2 = shift_z(dressed, -2)
    other = lax.ppermute(own, "zh", SWAP)
    dressed = jnp.concatenate([dressed, below_2, above_2, below_4, above_4])
    dressed_next = shift_z(dressed, 1)
    dressed = spread(jnp.stack([dressed, dressed_next]), "x").reshape(-1, virt)
    tau = lax.dynamic_update_index_in_dim(tau, other, 1 - zh, 0)
    below = lax.ppermute(tau, "y", UP)
    above = lax.ppermute(tau, "y", DOWN)
    far = lax.ppermute(below, "y", UP)
    dressed_other = lax.ppermute(dressed, "k", SWAP)
    taus = (tau, above, far, below)
    parts = ladder(dressed, taus)
    parts = ladder(dressed_other, taus, parts, doubles)
    parts = exchange(parts, AUX)
    return last(parts, denominator)[:, None, :]


def solution(mesh):
    fine = Mesh(mesh.devices.reshape(8, 4, 2, 4, 2), PAIR + AUX)
    placed = (
        P(PAIR, AUX, None),
        P(),
        P(AUX + PAIR, None, None),
        P(AUX + PAIR, None, None),
        P(),
        P(),
        P(PAIR, None),
    )
    return jax.shard_map(
        body, mesh=fine, in_specs=placed, out_specs=P(PAIR, AUX, None), check_vma=False
    )
```

```python
import functools

import jax
import jax.numpy as jnp
from jax import lax
from jax.experimental import pallas as pl
from jax.experimental.pallas import tpu as pltpu
from jax.sharding import Mesh, PartitionSpec as P


NWIN = 8
GROUP = 256
PAIR = ("zm", "zb", "x", "k")
AUX = ("y", "zh")
SWAP = [(0, 1), (1, 0)]
UP = [(i, (i + 1) % 4) for i in range(4)]
DOWN = [(i, (i + 3) % 4) for i in range(4)]
SMEM = pl.BlockSpec(memory_space=pltpu.SMEM)
VMEM = pl.BlockSpec(memory_space=pltpu.VMEM)


def start_kernel(
    pairs_ref, occ_energy_ref, vir_energy_ref, doubles_ref, singles_ref, vir_ref, occ_ref,
    dressed_ref, own_ref, tau_ref, denominator_ref, cols_ref,
):
    local_pairs, chunk, _ = doubles_ref.shape
    zh = lax.axis_index("zh")
    aux = lax.axis_index("y") * 2 + zh
    singles = singles_ref[...]
    occ = singles.shape[0]
    window = singles[:, :128].astype(jnp.float32).T[:NWIN].astype(jnp.bfloat16)
    for slab in range(occ_ref.shape[0]):
        dressed = vir_ref[slab].astype(jnp.float32) - jnp.dot(
            window, occ_ref[slab], preferred_element_type=jnp.float32
        )
        dressed = dressed.astype(jnp.bfloat16)
        for copy in range(dressed_ref.shape[0]):
            dressed_ref[copy, slab * NWIN : (slab + 1) * NWIN, :] = dressed
    ids = lax.broadcasted_iota(jnp.int32, (occ, 128), 0)
    lane = lax.broadcasted_iota(jnp.int32, (occ, 128), 1)
    first = jnp.zeros((occ, 128), jnp.float32)
    for pair in range(local_pairs):
        first = jnp.where((lane == pair) & (ids == pairs_ref[pair, 0]), 1.0, first)
    cols_ref[...] = lax.dot_general(
        singles, first.astype(jnp.bfloat16), (((0,), (0,)), ((), ())), preferred_element_type=jnp.float32
    )
    cols = cols_ref[pl.ds(pl.multiple_of(aux * chunk, chunk), chunk), :]
    ids = lax.broadcasted_iota(jnp.int32, (16, occ), 1)
    row = lax.broadcasted_iota(jnp.int32, (16, occ), 0)
    second = jnp.zeros((16, occ), jnp.float32)
    for pair in range(local_pairs):
        second = jnp.where((row == pair) & (ids == pairs_ref[pair, 1]), 1.0, second)
    rows = jnp.dot(second.astype(jnp.bfloat16), singles, preferred_element_type=jnp.float32)
    for pair in range(local_pairs):
        outer = cols[:, pair : pair + 1] * rows[pair : pair + 1, :]
        tau = (doubles_ref[pair].astype(jnp.float32) + outer).astype(jnp.bfloat16)
        own_ref[pair] = tau
        tau_ref[zh, pair] = tau
    lane = lax.broadcasted_iota(jnp.int32, (1, 128), 1)
    vir = jnp.zeros((1, 128), jnp.float32)
    for b in range(NWIN):
        vir = jnp.where(lane == b, vir_energy_ref[b], vir)
    for pair in range(local_pairs):
        energy = occ_energy_ref[pairs_ref[pair, 0]] + occ_energy_ref[pairs_ref[pair, 1]]
        value = (energy - vir_energy_ref[aux]) - vir
        denominator_ref[pair : pair + 1] = jnp.where(lane < NWIN, value, 1.0)


def start(doubles, singles, vir_slabs, occ_slabs, occ_energy, vir_energy, pair_list):
    local_pairs, chunk, virt = doubles.shape
    slabs, occ, _ = occ_slabs.shape
    return pl.pallas_call(
        start_kernel,
        out_shape=(
            jax.ShapeDtypeStruct((4, slabs * NWIN, virt), jnp.bfloat16),
            jax.ShapeDtypeStruct((local_pairs, chunk, virt), jnp.bfloat16),
            jax.ShapeDtypeStruct((2, local_pairs, chunk, virt), jnp.bfloat16),
            jax.ShapeDtypeStruct((local_pairs, 128), jnp.float32),
        ),
        in_specs=[SMEM] * 3 + [VMEM] * 4,
        out_specs=(VMEM,) * 4,
        scratch_shapes=[pltpu.VMEM((virt, 128), jnp.float32)],
        cost_estimate=pl.CostEstimate(flops=slabs * NWIN * occ * virt * 2, bytes_accessed=3 << 20, transcendentals=0),
        name="start",
    )(pair_list, occ_energy, vir_energy, doubles, singles, vir_slabs, occ_slabs)


def fold(gram):
    row = lax.broadcasted_iota(jnp.int32, (GROUP, GROUP), 0) // NWIN
    col = lax.broadcasted_iota(jnp.int32, (GROUP, GROUP), 1) // NWIN
    kept = jnp.where(row == col, gram, 0.0)
    folded = jnp.sum(kept.reshape(GROUP // NWIN, NWIN, GROUP), axis=0)
    folded = folded[:, :128] + folded[:, 128:]
    shift = 64
    while shift >= NWIN:
        folded = folded + pltpu.roll(folded, shift, 1)
        shift //= 2
    return folded


def ladder_kernel(slab_count, has_earlier, pays, *refs):
    slab_refs, refs = refs[:slab_count], refs[slab_count:]
    tau_refs, refs = refs[:2], refs[2:]
    earlier_ref = refs[0] if has_earlier else None
    doubles_ref = refs[1] if pays else None
    out_ref = refs[-1]
    pairs, virt = tau_refs[0].shape[2], tau_refs[0].shape[4]
    core = lax.axis_index("k")
    lane = lax.broadcasted_iota(jnp.int32, (NWIN, 128), 1)
    holds = (lax.axis_index("y") == 0) & (lax.axis_index("zh") == 0)
    for owner, tau_ref in enumerate(tau_refs):
        for pair in range(pairs):
            tau = tau_ref[:, :, pair].reshape(virt, virt)
            gram = None
            for slab_ref in slab_refs:
                slabs = slab_ref[...]
                half = jnp.dot(slabs, tau, preferred_element_type=jnp.float32).astype(jnp.bfloat16)
                for at in range(0, slabs.shape[0], GROUP):
                    block = lax.dot_general(
                        half[at : at + GROUP],
                        slabs[at : at + GROUP],
                        (((1,), (1,)), ((), ())),
                        preferred_element_type=jnp.float32,
                    )
                    gram = block if gram is None else gram + block
            residual = fold(gram)
            if has_earlier:
                residual = residual + earlier_ref[owner * pairs + pair]
            if not pays:
                out_ref[owner * pairs + pair] = residual
                continue
            row = jnp.where(lane < NWIN, residual, 0.0)
            if owner == 0:
                doubles = pltpu.roll(doubles_ref[pair].astype(jnp.float32)[:NWIN], NWIN, 1)
                doubles = jnp.where((lane < 2 * NWIN) & holds, doubles, 0.0)
                row = jnp.where(lane < NWIN, residual, doubles)
            to = core if owner == 0 else 1 - core
            for a in range(NWIN):
                out_ref[to * NWIN + a, pair : pair + 1, :] = row[a : a + 1]


def ladder(slabs, taus, earlier=None, doubles=None):
    pairs, virt = taus[0].shape[2], taus[0].shape[4]
    rows = sum(slab.shape[0] for slab in slabs)
    has_earlier, pays = earlier is not None, doubles is not None
    specs, operands = [VMEM] * (len(slabs) + 2), [*slabs, *taus]
    out = (2 * pairs, NWIN, 128)
    if has_earlier:
        specs.append(VMEM)
        operands.append(earlier)
    if pays:
        specs.append(pl.BlockSpec((pairs, 16, 128), lambda i: (0, 0, 0)))
        operands.append(doubles)
        out = (2 * NWIN, pairs, 128)
    return pl.pallas_call(
        functools.partial(ladder_kernel, len(slabs), has_earlier, pays),
        out_shape=jax.ShapeDtypeStruct(out, jnp.float32),
        grid=(1,),
        in_specs=specs,
        out_specs=VMEM,
        cost_estimate=pl.CostEstimate(
            flops=2 * pairs * rows * virt * (virt + GROUP) * 2,
            bytes_accessed=2 * rows * virt + 4 * pairs * virt * virt,
            transcendentals=0,
        ),
        compiler_params=pltpu.CompilerParams(vmem_limit_bytes=24 << 20),
        name="ladder",
    )(*operands)


def last_kernel(parts_ref, denominator_ref, out_ref):
    total = jnp.sum(parts_ref[...], axis=0)
    value = pltpu.roll(total, 128 - NWIN, 1) + total / denominator_ref[...]
    out_ref[...] = value[:, :NWIN]


def last(parts, denominator):
    return pl.pallas_call(
        last_kernel,
        out_shape=jax.ShapeDtypeStruct((parts.shape[1], NWIN), jnp.float32),
        in_specs=[VMEM, VMEM],
        out_specs=VMEM,
        name="last",
    )(parts, denominator)


def exchange(copies, axis):
    return lax.all_to_all(copies, axis, split_axis=0, concat_axis=0, tiled=True)


def spread(value, axis):
    return exchange(jnp.broadcast_to(value[None], (lax.axis_size(axis),) + value.shape), axis)


def body(doubles, singles, vir_slabs, occ_slabs, occ_energy, vir_energy, pair_list):
    virt = doubles.shape[2]
    zh = lax.axis_index("zh")
    copies, own, tau, denominator = start(
        doubles, singles, vir_slabs, occ_slabs, occ_energy, vir_energy, pair_list
    )
    dressed = exchange(copies, "zm").reshape(-1, virt)
    other = lax.ppermute(own, "zh", SWAP)
    dressed_next = lax.ppermute(dressed, "zb", SWAP)
    tau = lax.dynamic_update_index_in_dim(tau, other, 1 - zh, 0)
    tau = spread(tau, "y")
    mine = jnp.concatenate([dressed, dressed_next])
    below = lax.ppermute(mine, "x", UP)
    above = lax.ppermute(mine, "x", DOWN)
    tau_other = lax.ppermute(tau, "k", SWAP)
    far_up = lax.ppermute(below[: dressed.shape[0]], "x", UP)
    far_down = lax.ppermute(above[dressed.shape[0] :], "x", DOWN)
    taus = (tau, tau_other)
    parts = ladder((mine,), taus)
    parts = ladder((below, above), taus, parts)
    parts = ladder((far_up, far_down), taus, parts, doubles)
    parts = exchange(parts, ("k",) + AUX)
    return last(parts, denominator)[:, None, :]


def solution(mesh):
    fine = Mesh(mesh.devices.reshape(4, 2, 4, 2, 4, 2), PAIR + AUX)
    placed = (
        P(PAIR, AUX, None),
        P(),
        P(AUX + PAIR, None, None),
        P(AUX + PAIR, None, None),
        P(),
        P(),
        P(PAIR, None),
    )
    return jax.shard_map(
        body, mesh=fine, in_specs=placed, out_specs=P(PAIR, AUX, None), check_vma=False
    )
```

```python
import functools

import jax
import jax.numpy as jnp
from jax import lax
from jax.experimental import pallas as pl
from jax.experimental.pallas import tpu as pltpu
from jax.sharding import Mesh, PartitionSpec as P


NWIN = 8
GROUP = 256
PAIR = ("zm", "zb", "x", "k")
AUX = ("y", "zh")
SWAP = [(0, 1), (1, 0)]
UP = [(i, (i + 1) % 4) for i in range(4)]
DOWN = [(i, (i + 3) % 4) for i in range(4)]
SMEM = pl.BlockSpec(memory_space=pltpu.SMEM)
VMEM = pl.BlockSpec(memory_space=pltpu.VMEM)


def start_kernel(
    pairs_ref, occ_energy_ref, vir_energy_ref, doubles_ref, singles_ref, vir_ref, occ_ref,
    dressed_ref, own_ref, denominator_ref, cols_ref,
):
    local_pairs, chunk, _ = doubles_ref.shape
    aux = lax.axis_index("y") * 2 + lax.axis_index("zh")
    singles = singles_ref[...]
    occ = singles.shape[0]
    window = singles[:, :128].astype(jnp.float32).T[:NWIN].astype(jnp.bfloat16)
    for slab in range(occ_ref.shape[0]):
        dressed = vir_ref[slab].astype(jnp.float32) - jnp.dot(
            window, occ_ref[slab], preferred_element_type=jnp.float32
        )
        dressed = dressed.astype(jnp.bfloat16)
        for copy in range(dressed_ref.shape[0]):
            dressed_ref[copy, slab * NWIN : (slab + 1) * NWIN, :] = dressed
    ids = lax.broadcasted_iota(jnp.int32, (occ, 128), 0)
    lane = lax.broadcasted_iota(jnp.int32, (occ, 128), 1)
    first = jnp.zeros((occ, 128), jnp.float32)
    for pair in range(local_pairs):
        first = jnp.where((lane == pair) & (ids == pairs_ref[pair, 0]), 1.0, first)
    cols_ref[...] = lax.dot_general(
        singles, first.astype(jnp.bfloat16), (((0,), (0,)), ((), ())), preferred_element_type=jnp.float32
    )
    cols = cols_ref[pl.ds(pl.multiple_of(aux * chunk, chunk), chunk), :]
    ids = lax.broadcasted_iota(jnp.int32, (16, occ), 1)
    row = lax.broadcasted_iota(jnp.int32, (16, occ), 0)
    second = jnp.zeros((16, occ), jnp.float32)
    for pair in range(local_pairs):
        second = jnp.where((row == pair) & (ids == pairs_ref[pair, 1]), 1.0, second)
    rows = jnp.dot(second.astype(jnp.bfloat16), singles, preferred_element_type=jnp.float32)
    for pair in range(local_pairs):
        outer = cols[:, pair : pair + 1] * rows[pair : pair + 1, :]
        tau = (doubles_ref[pair].astype(jnp.float32) + outer).astype(jnp.bfloat16)
        own_ref[pair] = tau
    lane = lax.broadcasted_iota(jnp.int32, (1, 128), 1)
    vir = jnp.zeros((1, 128), jnp.float32)
    for b in range(NWIN):
        vir = jnp.where(lane == b, vir_energy_ref[b], vir)
    for pair in range(local_pairs):
        energy = occ_energy_ref[pairs_ref[pair, 0]] + occ_energy_ref[pairs_ref[pair, 1]]
        value = (energy - vir_energy_ref[aux]) - vir
        denominator_ref[pair : pair + 1] = jnp.where(lane < NWIN, value, 0.0)


def start(doubles, singles, vir_slabs, occ_slabs, occ_energy, vir_energy, pair_list):
    local_pairs, chunk, virt = doubles.shape
    slabs, occ, _ = occ_slabs.shape
    return pl.pallas_call(
        start_kernel,
        out_shape=(
            jax.ShapeDtypeStruct((4, slabs * NWIN, virt), jnp.bfloat16),
            jax.ShapeDtypeStruct((local_pairs, chunk, virt), jnp.bfloat16),
            jax.ShapeDtypeStruct((local_pairs, 128), jnp.float32),
        ),
        in_specs=[SMEM] * 3 + [VMEM] * 4,
        out_specs=(VMEM,) * 3,
        scratch_shapes=[pltpu.VMEM((virt, 128), jnp.float32)],
        cost_estimate=pl.CostEstimate(flops=slabs * NWIN * occ * virt * 2, bytes_accessed=3 << 20, transcendentals=0),
        name="start",
    )(pair_list, occ_energy, vir_energy, doubles, singles, vir_slabs, occ_slabs)


def fold(gram):
    row = lax.broadcasted_iota(jnp.int32, (GROUP, GROUP), 0) // NWIN
    col = lax.broadcasted_iota(jnp.int32, (GROUP, GROUP), 1) // NWIN
    kept = jnp.where(row == col, gram, 0.0)
    folded = jnp.sum(kept.reshape(GROUP // NWIN, NWIN, GROUP), axis=0)
    folded = folded[:, :128] + folded[:, 128:]
    shift = 64
    while shift >= NWIN:
        folded = folded + pltpu.roll(folded, shift, 1)
        shift //= 2
    return folded


def ladder_kernel(slab_count, has_earlier, pays, *refs):
    slab_refs, refs = refs[:slab_count], refs[slab_count:]
    tau_refs, refs = refs[:2], refs[2:]
    earlier_ref = refs[0] if has_earlier else None
    doubles_ref = refs[1] if pays else None
    out_ref = refs[-1]
    pairs, virt = tau_refs[0].shape[2], tau_refs[0].shape[4]
    core = lax.axis_index("k")
    lane = lax.broadcasted_iota(jnp.int32, (NWIN, 128), 1)
    holds = (lax.axis_index("y") == 0) & (lax.axis_index("zh") == 0)
    for owner, tau_ref in enumerate(tau_refs):
        for pair in range(pairs):
            tau = tau_ref[:, :, pair].reshape(virt, virt)
            gram = None
            for slab_ref in slab_refs:
                slabs = slab_ref[...]
                half = jnp.dot(slabs, tau, preferred_element_type=jnp.float32).astype(jnp.bfloat16)
                for at in range(0, slabs.shape[0], GROUP):
                    block = lax.dot_general(
                        half[at : at + GROUP],
                        slabs[at : at + GROUP],
                        (((1,), (1,)), ((), ())),
                        preferred_element_type=jnp.float32,
                    )
                    gram = block if gram is None else gram + block
            residual = fold(gram)
            if has_earlier:
                residual = residual + earlier_ref[owner * pairs + pair]
            if not pays:
                out_ref[owner * pairs + pair] = residual
                continue
            row = jnp.where(lane < NWIN, residual, 0.0)
            if owner == 0:
                doubles = pltpu.roll(doubles_ref[pair].astype(jnp.float32)[:NWIN], NWIN, 1)
                doubles = jnp.where((lane < 2 * NWIN) & holds, doubles, 0.0)
                row = jnp.where(lane < NWIN, residual, doubles)
            to = core if owner == 0 else 1 - core
            for a in range(NWIN):
                out_ref[to * NWIN + a, pair : pair + 1, :] = row[a : a + 1]


def ladder(slabs, taus, earlier=None, doubles=None):
    pairs, virt = taus[0].shape[2], taus[0].shape[4]
    rows = sum(slab.shape[0] for slab in slabs)
    has_earlier, pays = earlier is not None, doubles is not None
    specs, operands = [VMEM] * (len(slabs) + 2), [*slabs, *taus]
    out = (2 * pairs, NWIN, 128)
    if has_earlier:
        specs.append(VMEM)
        operands.append(earlier)
    if pays:
        specs.append(pl.BlockSpec((pairs, 16, 128), lambda i: (0, 0, 0)))
        operands.append(doubles)
        out = (2 * NWIN, pairs, 128)
    return pl.pallas_call(
        functools.partial(ladder_kernel, len(slabs), has_earlier, pays),
        out_shape=jax.ShapeDtypeStruct(out, jnp.float32),
        grid=(1,),
        in_specs=specs,
        out_specs=VMEM,
        cost_estimate=pl.CostEstimate(
            flops=2 * pairs * rows * virt * (virt + GROUP) * 2,
            bytes_accessed=2 * rows * virt + 4 * pairs * virt * virt,
            transcendentals=0,
        ),
        compiler_params=pltpu.CompilerParams(vmem_limit_bytes=24 << 20),
        name="ladder",
    )(*operands)


def join_kernel(own_ref, other_ref, out_ref):
    zh = lax.axis_index("zh")
    for copy in range(out_ref.shape[0]):
        out_ref[copy, zh] = own_ref[...]
        out_ref[copy, 1 - zh] = other_ref[...]


def join(own, other):
    return pl.pallas_call(
        join_kernel,
        out_shape=jax.ShapeDtypeStruct((4, 2) + own.shape, own.dtype),
        in_specs=[VMEM, VMEM],
        out_specs=VMEM,
        compiler_params=pltpu.CompilerParams(vmem_limit_bytes=6 << 20),
        name="join",
    )(own, other)


def exchange(copies, axis):
    return lax.all_to_all(copies, axis, split_axis=0, concat_axis=0, tiled=True)


def body(doubles, singles, vir_slabs, occ_slabs, occ_energy, vir_energy, pair_list):
    virt = doubles.shape[2]
    copies, own, denominator = start(
        doubles, singles, vir_slabs, occ_slabs, occ_energy, vir_energy, pair_list
    )
    dressed = exchange(copies, "zm").reshape(-1, virt)
    other = lax.ppermute(own, "zh", SWAP)
    dressed_next = lax.ppermute(dressed, "zb", SWAP)
    copies = join(own, other)
    tau = exchange(copies, "y")
    mine = jnp.concatenate([dressed, dressed_next])
    below = lax.ppermute(mine, "x", UP)
    above = lax.ppermute(mine, "x", DOWN)
    tau_other = lax.ppermute(tau, "k", SWAP)
    far_up = lax.ppermute(below[: dressed.shape[0]], "x", UP)
    far_down = lax.ppermute(above[dressed.shape[0] :], "x", DOWN)
    denominator = lax.optimization_barrier(denominator[:, :NWIN] + denominator[:, 64 : 64 + NWIN])
    taus = (tau, tau_other)
    parts = ladder((mine,), taus)
    parts = ladder((below, above), taus, parts)
    parts = ladder((far_up, far_down), taus, parts, doubles)
    parts = exchange(parts, ("k",) + AUX)
    total = jnp.sum(parts, axis=0)
    residual = total[:, :NWIN] / denominator
    return (total[:, NWIN : 2 * NWIN] + residual)[:, None, :]


def solution(mesh):
    fine = Mesh(mesh.devices.reshape(4, 2, 4, 2, 4, 2), PAIR + AUX)
    placed = (
        P(PAIR, AUX, None),
        P(),
        P(AUX + PAIR, None, None),
        P(AUX + PAIR, None, None),
        P(),
        P(),
        P(PAIR, None),
    )
    return jax.shard_map(
        body, mesh=fine, in_specs=placed, out_specs=P(PAIR, AUX, None), check_vma=False
    )
```

```python
import functools

import jax
import jax.numpy as jnp
from jax import lax
from jax.experimental import pallas as pl
from jax.experimental.pallas import tpu as pltpu
from jax.sharding import Mesh, PartitionSpec as P


NWIN = 8
GROUP = 256
PAIR = ("zm", "zb", "x", "k")
AUX = ("y", "zh")
SWAP = [(0, 1), (1, 0)]
UP = [(i, (i + 1) % 4) for i in range(4)]
DOWN = [(i, (i + 3) % 4) for i in range(4)]
SMEM = pl.BlockSpec(memory_space=pltpu.SMEM)
VMEM = pl.BlockSpec(memory_space=pltpu.VMEM)


def start_kernel(
    pairs_ref, occ_energy_ref, vir_energy_ref, doubles_ref, singles_ref, vir_ref, occ_ref,
    dressed_ref, own_ref, denominator_ref, cols_ref,
):
    local_pairs, chunk, _ = doubles_ref.shape
    aux = lax.axis_index("y") * 2 + lax.axis_index("zh")
    singles = singles_ref[...]
    occ = singles.shape[0]
    window = singles[:, :128].astype(jnp.float32).T[:NWIN].astype(jnp.bfloat16)
    for slab in range(occ_ref.shape[0]):
        dressed = vir_ref[slab].astype(jnp.float32) - jnp.dot(
            window, occ_ref[slab], preferred_element_type=jnp.float32
        )
        dressed = dressed.astype(jnp.bfloat16)
        for copy in range(dressed_ref.shape[0]):
            dressed_ref[copy, slab * NWIN : (slab + 1) * NWIN, :] = dressed
    ids = lax.broadcasted_iota(jnp.int32, (occ, 128), 0)
    lane = lax.broadcasted_iota(jnp.int32, (occ, 128), 1)
    first = jnp.zeros((occ, 128), jnp.float32)
    for pair in range(local_pairs):
        first = jnp.where((lane == pair) & (ids == pairs_ref[pair, 0]), 1.0, first)
    cols_ref[...] = lax.dot_general(
        singles, first.astype(jnp.bfloat16), (((0,), (0,)), ((), ())), preferred_element_type=jnp.float32
    )
    cols = cols_ref[pl.ds(pl.multiple_of(aux * chunk, chunk), chunk), :]
    ids = lax.broadcasted_iota(jnp.int32, (16, occ), 1)
    row = lax.broadcasted_iota(jnp.int32, (16, occ), 0)
    second = jnp.zeros((16, occ), jnp.float32)
    for pair in range(local_pairs):
        second = jnp.where((row == pair) & (ids == pairs_ref[pair, 1]), 1.0, second)
    rows = jnp.dot(second.astype(jnp.bfloat16), singles, preferred_element_type=jnp.float32)
    for pair in range(local_pairs):
        outer = cols[:, pair : pair + 1] * rows[pair : pair + 1, :]
        tau = (doubles_ref[pair].astype(jnp.float32) + outer).astype(jnp.bfloat16)
        own_ref[pair] = tau
    lane = lax.broadcasted_iota(jnp.int32, (1, 128), 1)
    vir = jnp.zeros((1, 128), jnp.float32)
    for b in range(NWIN):
        vir = jnp.where(lane == b, vir_energy_ref[b], vir)
    for pair in range(local_pairs):
        energy = occ_energy_ref[pairs_ref[pair, 0]] + occ_energy_ref[pairs_ref[pair, 1]]
        value = (energy - vir_energy_ref[aux]) - vir
        denominator_ref[pair : pair + 1] = jnp.where(lane < NWIN, value, 0.0)


def start(doubles, singles, vir_slabs, occ_slabs, occ_energy, vir_energy, pair_list):
    local_pairs, chunk, virt = doubles.shape
    slabs, occ, _ = occ_slabs.shape
    return pl.pallas_call(
        start_kernel,
        out_shape=(
            jax.ShapeDtypeStruct((4, slabs * NWIN, virt), jnp.bfloat16),
            jax.ShapeDtypeStruct((local_pairs, chunk, virt), jnp.bfloat16),
            jax.ShapeDtypeStruct((local_pairs, 128), jnp.float32),
        ),
        in_specs=[SMEM] * 3 + [VMEM] * 4,
        out_specs=(VMEM,) * 3,
        scratch_shapes=[pltpu.VMEM((virt, 128), jnp.float32)],
        cost_estimate=pl.CostEstimate(flops=slabs * NWIN * occ * virt * 2, bytes_accessed=3 << 20, transcendentals=0),
        name="start",
    )(pair_list, occ_energy, vir_energy, doubles, singles, vir_slabs, occ_slabs)


def fold(gram):
    row = lax.broadcasted_iota(jnp.int32, (GROUP, GROUP), 0) // NWIN
    col = lax.broadcasted_iota(jnp.int32, (GROUP, GROUP), 1) // NWIN
    kept = jnp.where(row == col, gram, 0.0)
    folded = jnp.sum(kept.reshape(GROUP // NWIN, NWIN, GROUP), axis=0)
    folded = folded[:, :128] + folded[:, 128:]
    shift = 64
    while shift >= NWIN:
        folded = folded + pltpu.roll(folded, shift, 1)
        shift //= 2
    return folded


def slab_blocks(slab_refs):
    for ref in slab_refs:
        if len(ref.shape) == 2:
            yield ref[...]
            continue
        for step in range(1, ref.shape[0]):
            yield ref[lax.rem(lax.axis_index("x") + step, ref.shape[0])]


def ladder_kernel(slab_count, has_earlier, pays, *refs):
    slab_refs, refs = refs[:slab_count], refs[slab_count:]
    tau_refs, refs = refs[:2], refs[2:]
    earlier_ref = refs[0] if has_earlier else None
    doubles_ref = refs[1] if pays else None
    out_ref = refs[-1]
    pairs, virt = tau_refs[0].shape[2], tau_refs[0].shape[4]
    core = lax.axis_index("k")
    lane = lax.broadcasted_iota(jnp.int32, (NWIN, 128), 1)
    holds = (lax.axis_index("y") == 0) & (lax.axis_index("zh") == 0)
    for owner, tau_ref in enumerate(tau_refs):
        for pair in range(pairs):
            tau = tau_ref[:, :, pair].reshape(virt, virt)
            gram = None
            for slabs in slab_blocks(slab_refs):
                half = jnp.dot(slabs, tau, preferred_element_type=jnp.float32).astype(jnp.bfloat16)
                for at in range(0, slabs.shape[0], GROUP):
                    block = lax.dot_general(
                        half[at : at + GROUP],
                        slabs[at : at + GROUP],
                        (((1,), (1,)), ((), ())),
                        preferred_element_type=jnp.float32,
                    )
                    gram = block if gram is None else gram + block
            residual = fold(gram)
            if has_earlier:
                residual = residual + earlier_ref[owner * pairs + pair]
            if not pays:
                out_ref[owner * pairs + pair] = residual
                continue
            row = jnp.where(lane < NWIN, residual, 0.0)
            if owner == 0:
                doubles = pltpu.roll(doubles_ref[pair].astype(jnp.float32)[:NWIN], NWIN, 1)
                doubles = jnp.where((lane < 2 * NWIN) & holds, doubles, 0.0)
                row = jnp.where(lane < NWIN, residual, doubles)
            to = core if owner == 0 else 1 - core
            for a in range(NWIN):
                out_ref[to * NWIN + a, pair : pair + 1, :] = row[a : a + 1]


def ladder(slabs, taus, earlier=None, doubles=None):
    pairs, virt = taus[0].shape[2], taus[0].shape[4]
    rows = sum(slab.size // virt for slab in slabs)
    has_earlier, pays = earlier is not None, doubles is not None
    specs, operands = [VMEM] * (len(slabs) + 2), [*slabs, *taus]
    out = (2 * pairs, NWIN, 128)
    if has_earlier:
        specs.append(VMEM)
        operands.append(earlier)
    if pays:
        specs.append(pl.BlockSpec((pairs, 16, 128), lambda i: (0, 0, 0)))
        operands.append(doubles)
        out = (2 * NWIN, pairs, 128)
    return pl.pallas_call(
        functools.partial(ladder_kernel, len(slabs), has_earlier, pays),
        out_shape=jax.ShapeDtypeStruct(out, jnp.float32),
        grid=(1,),
        in_specs=specs,
        out_specs=VMEM,
        cost_estimate=pl.CostEstimate(
            flops=2 * pairs * rows * virt * (virt + GROUP) * 2,
            bytes_accessed=2 * rows * virt + 4 * pairs * virt * virt,
            transcendentals=0,
        ),
        compiler_params=pltpu.CompilerParams(vmem_limit_bytes=24 << 20),
        name="ladder",
    )(*operands)


def join_kernel(own_ref, other_ref, out_ref):
    zh = lax.axis_index("zh")
    out_ref[zh] = own_ref[...]
    out_ref[1 - zh] = other_ref[...]


def join(own, other):
    return pl.pallas_call(
        join_kernel,
        out_shape=jax.ShapeDtypeStruct((2,) + own.shape, own.dtype),
        in_specs=[VMEM, VMEM],
        out_specs=VMEM,
        compiler_params=pltpu.CompilerParams(vmem_limit_bytes=4 << 20),
        name="join",
    )(own, other)


def assemble_kernel(own_ref, above_ref, far_ref, below_ref, out_ref):
    y = lax.axis_index("y")
    for step, ref in enumerate((own_ref, above_ref, far_ref, below_ref)):
        out_ref[lax.rem(y + step, 4)] = ref[...]


def assemble(own, above, far, below):
    return pl.pallas_call(
        assemble_kernel,
        out_shape=jax.ShapeDtypeStruct((4,) + own.shape, own.dtype),
        in_specs=[VMEM] * 4,
        out_specs=VMEM,
        compiler_params=pltpu.CompilerParams(vmem_limit_bytes=6 << 20),
        name="assemble",
    )(own, above, far, below)


def exchange(copies, axis):
    return lax.all_to_all(copies, axis, split_axis=0, concat_axis=0, tiled=True)


def body(doubles, singles, vir_slabs, occ_slabs, occ_energy, vir_energy, pair_list):
    virt = doubles.shape[2]
    copies, own, denominator = start(
        doubles, singles, vir_slabs, occ_slabs, occ_energy, vir_energy, pair_list
    )
    dressed = exchange(copies, "zm").reshape(-1, virt)
    other = lax.ppermute(own, "zh", SWAP)
    dressed_next = lax.ppermute(dressed, "zb", SWAP)
    tau = join(own, other)
    below = lax.ppermute(tau, "y", UP)
    above = lax.ppermute(tau, "y", DOWN)
    far = lax.ppermute(below, "y", UP)
    mine = jnp.concatenate([dressed, dressed_next])
    slabs = exchange(jnp.broadcast_to(mine[None], (4,) + mine.shape), "x")
    tau = assemble(tau, above, far, below)
    tau_other = lax.ppermute(tau, "k", SWAP)
    taus = (tau, tau_other)
    parts = ladder((mine,), taus)
    parts = ladder((slabs,), taus, parts, doubles)
    parts = exchange(parts, ("k",) + AUX)
    total = jnp.sum(parts, axis=0)
    residual = total[:, :NWIN] / denominator[:, :NWIN]
    return (total[:, NWIN : 2 * NWIN] + residual)[:, None, :]


def solution(mesh):
    fine = Mesh(mesh.devices.reshape(4, 2, 4, 2, 4, 2), PAIR + AUX)
    placed = (
        P(PAIR, AUX, None),
        P(),
        P(AUX + PAIR, None, None),
        P(AUX + PAIR, None, None),
        P(),
        P(),
        P(PAIR, None),
    )
    return jax.shard_map(
        body, mesh=fine, in_specs=placed, out_specs=P(PAIR, AUX, None), check_vma=False
    )
```

```python
import functools

import jax
import jax.numpy as jnp
from jax import lax
from jax.experimental import pallas as pl
from jax.experimental.pallas import tpu as pltpu
from jax.sharding import Mesh, PartitionSpec as P


NWIN = 8
GROUP = 256
PAIR = ("zm", "zb", "x", "k")
AUX = ("y", "zh")
SWAP = [(0, 1), (1, 0)]
UP = [(i, (i + 1) % 4) for i in range(4)]
DOWN = [(i, (i + 3) % 4) for i in range(4)]
FAR = [(i, (i + 2) % 4) for i in range(4)]
SMEM = pl.BlockSpec(memory_space=pltpu.SMEM)
VMEM = pl.BlockSpec(memory_space=pltpu.VMEM)


def start_kernel(
    pairs_ref, occ_energy_ref, vir_energy_ref, doubles_ref, singles_ref, vir_ref, occ_ref,
    dressed_ref, own_ref, denominator_ref, cols_ref,
):
    local_pairs, chunk, _ = doubles_ref.shape
    aux = lax.axis_index("y") * 2 + lax.axis_index("zh")
    singles = singles_ref[...]
    occ = singles.shape[0]
    window = singles[:, :128].astype(jnp.float32).T[:NWIN].astype(jnp.bfloat16)
    for slab in range(occ_ref.shape[0]):
        dressed = vir_ref[slab].astype(jnp.float32) - jnp.dot(
            window, occ_ref[slab], preferred_element_type=jnp.float32
        )
        dressed = dressed.astype(jnp.bfloat16)
        for copy in range(dressed_ref.shape[0]):
            dressed_ref[copy, slab * NWIN : (slab + 1) * NWIN, :] = dressed
    ids = lax.broadcasted_iota(jnp.int32, (occ, 128), 0)
    lane = lax.broadcasted_iota(jnp.int32, (occ, 128), 1)
    first = jnp.zeros((occ, 128), jnp.float32)
    for pair in range(local_pairs):
        first = jnp.where((lane == pair) & (ids == pairs_ref[pair, 0]), 1.0, first)
    cols_ref[...] = lax.dot_general(
        singles, first.astype(jnp.bfloat16), (((0,), (0,)), ((), ())), preferred_element_type=jnp.float32
    )
    cols = cols_ref[pl.ds(pl.multiple_of(aux * chunk, chunk), chunk), :]
    ids = lax.broadcasted_iota(jnp.int32, (16, occ), 1)
    row = lax.broadcasted_iota(jnp.int32, (16, occ), 0)
    second = jnp.zeros((16, occ), jnp.float32)
    for pair in range(local_pairs):
        second = jnp.where((row == pair) & (ids == pairs_ref[pair, 1]), 1.0, second)
    rows = jnp.dot(second.astype(jnp.bfloat16), singles, preferred_element_type=jnp.float32)
    for pair in range(local_pairs):
        outer = cols[:, pair : pair + 1] * rows[pair : pair + 1, :]
        tau = (doubles_ref[pair].astype(jnp.float32) + outer).astype(jnp.bfloat16)
        own_ref[pair] = tau
    lane = lax.broadcasted_iota(jnp.int32, (1, 128), 1)
    vir = jnp.zeros((1, 128), jnp.float32)
    for b in range(NWIN):
        vir = jnp.where(lane == b, vir_energy_ref[b], vir)
    for pair in range(local_pairs):
        energy = occ_energy_ref[pairs_ref[pair, 0]] + occ_energy_ref[pairs_ref[pair, 1]]
        value = (energy - vir_energy_ref[aux]) - vir
        denominator_ref[pair : pair + 1] = jnp.where(lane < NWIN, value, 0.0)


def start(doubles, singles, vir_slabs, occ_slabs, occ_energy, vir_energy, pair_list):
    local_pairs, chunk, virt = doubles.shape
    slabs, occ, _ = occ_slabs.shape
    return pl.pallas_call(
        start_kernel,
        out_shape=(
            jax.ShapeDtypeStruct((4, slabs * NWIN, virt), jnp.bfloat16),
            jax.ShapeDtypeStruct((local_pairs, chunk, virt), jnp.bfloat16),
            jax.ShapeDtypeStruct((local_pairs, 128), jnp.float32),
        ),
        in_specs=[SMEM] * 3 + [VMEM] * 4,
        out_specs=(VMEM,) * 3,
        scratch_shapes=[pltpu.VMEM((virt, 128), jnp.float32)],
        cost_estimate=pl.CostEstimate(flops=slabs * NWIN * occ * virt * 2, bytes_accessed=3 << 20, transcendentals=0),
        name="start",
    )(pair_list, occ_energy, vir_energy, doubles, singles, vir_slabs, occ_slabs)


def fold(gram):
    row = lax.broadcasted_iota(jnp.int32, (GROUP, GROUP), 0) // NWIN
    col = lax.broadcasted_iota(jnp.int32, (GROUP, GROUP), 1) // NWIN
    kept = jnp.where(row == col, gram, 0.0)
    folded = jnp.sum(kept.reshape(GROUP // NWIN, NWIN, GROUP), axis=0)
    folded = folded[:, :128] + folded[:, 128:]
    shift = 64
    while shift >= NWIN:
        folded = folded + pltpu.roll(folded, shift, 1)
        shift //= 2
    return folded


def slab_blocks(slab_refs):
    for ref in slab_refs:
        if len(ref.shape) == 2:
            yield ref[...]
            continue
        for chip in range(ref.shape[0]):
            yield ref[chip]


def ladder_kernel(slab_count, has_earlier, pays, *refs):
    slab_refs, refs = refs[:slab_count], refs[slab_count:]
    tau_refs, refs = refs[:2], refs[2:]
    earlier_ref = refs[0] if has_earlier else None
    doubles_ref = refs[1] if pays else None
    out_ref = refs[-1]
    pairs, virt = tau_refs[0].shape[2], tau_refs[0].shape[4]
    core = lax.axis_index("k")
    lane = lax.broadcasted_iota(jnp.int32, (NWIN, 128), 1)
    holds = (lax.axis_index("y") == 0) & (lax.axis_index("zh") == 0)
    for owner, tau_ref in enumerate(tau_refs):
        for pair in range(pairs):
            tau = tau_ref[:, :, pair].reshape(virt, virt)
            gram = None
            for slabs in slab_blocks(slab_refs):
                half = jnp.dot(slabs, tau, preferred_element_type=jnp.float32).astype(jnp.bfloat16)
                for at in range(0, slabs.shape[0], GROUP):
                    block = lax.dot_general(
                        half[at : at + GROUP],
                        slabs[at : at + GROUP],
                        (((1,), (1,)), ((), ())),
                        preferred_element_type=jnp.float32,
                    )
                    gram = block if gram is None else gram + block
            residual = fold(gram)
            if has_earlier:
                residual = residual + earlier_ref[owner * pairs + pair]
            if not pays:
                out_ref[owner * pairs + pair] = residual
                continue
            row = jnp.where(lane < NWIN, residual, 0.0)
            if owner == 0:
                doubles = pltpu.roll(doubles_ref[pair].astype(jnp.float32)[:NWIN], NWIN, 1)
                doubles = jnp.where((lane < 2 * NWIN) & holds, doubles, 0.0)
                row = jnp.where(lane < NWIN, residual, doubles)
            to = core if owner == 0 else 1 - core
            for a in range(NWIN):
                out_ref[to * NWIN + a, pair : pair + 1, :] = row[a : a + 1]


def ladder(slabs, taus, earlier=None, doubles=None):
    pairs, virt = taus[0].shape[2], taus[0].shape[4]
    rows = sum(slab.size // virt for slab in slabs)
    has_earlier, pays = earlier is not None, doubles is not None
    specs, operands = [VMEM] * (len(slabs) + 2), [*slabs, *taus]
    out = (2 * pairs, NWIN, 128)
    if has_earlier:
        specs.append(VMEM)
        operands.append(earlier)
    if pays:
        specs.append(pl.BlockSpec((pairs, 16, 128), lambda i: (0, 0, 0)))
        operands.append(doubles)
        out = (2 * NWIN, pairs, 128)
    return pl.pallas_call(
        functools.partial(ladder_kernel, len(slabs), has_earlier, pays),
        out_shape=jax.ShapeDtypeStruct(out, jnp.float32),
        grid=(1,),
        in_specs=specs,
        out_specs=VMEM,
        cost_estimate=pl.CostEstimate(
            flops=2 * pairs * rows * virt * (virt + GROUP) * 2,
            bytes_accessed=2 * rows * virt + 4 * pairs * virt * virt,
            transcendentals=0,
        ),
        compiler_params=pltpu.CompilerParams(vmem_limit_bytes=24 << 20),
        name="ladder",
    )(*operands)


def join_kernel(own_ref, other_ref, out_ref):
    zh = lax.axis_index("zh")
    out_ref[zh] = own_ref[...]
    out_ref[1 - zh] = other_ref[...]


def join(own, other):
    return pl.pallas_call(
        join_kernel,
        out_shape=jax.ShapeDtypeStruct((2,) + own.shape, own.dtype),
        in_specs=[VMEM, VMEM],
        out_specs=VMEM,
        compiler_params=pltpu.CompilerParams(vmem_limit_bytes=4 << 20),
        name="join",
    )(own, other)


def assemble_kernel(own_ref, above_ref, far_ref, below_ref, out_ref):
    y = lax.axis_index("y")
    for step, ref in enumerate((own_ref, above_ref, far_ref, below_ref)):
        out_ref[lax.rem(y + step, 4)] = ref[...]


def assemble(own, above, far, below):
    return pl.pallas_call(
        assemble_kernel,
        out_shape=jax.ShapeDtypeStruct((4,) + own.shape, own.dtype),
        in_specs=[VMEM] * 4,
        out_specs=VMEM,
        compiler_params=pltpu.CompilerParams(vmem_limit_bytes=6 << 20),
        name="assemble",
    )(own, above, far, below)


def exchange(copies, axis):
    return lax.all_to_all(copies, axis, split_axis=0, concat_axis=0, tiled=True)


def body(doubles, singles, vir_slabs, occ_slabs, occ_energy, vir_energy, pair_list):
    virt = doubles.shape[2]
    copies, own, denominator = start(
        doubles, singles, vir_slabs, occ_slabs, occ_energy, vir_energy, pair_list
    )
    dressed = exchange(copies, "zm").reshape(-1, virt)
    other = lax.ppermute(own, "zh", SWAP)
    dressed_next = lax.ppermute(dressed, "zb", SWAP)
    tau = join(own, other)
    below = lax.ppermute(tau, "y", UP)
    above = lax.ppermute(tau, "y", DOWN)
    far = lax.ppermute(below, "y", UP)
    slabs = exchange(jnp.broadcast_to(dressed[None], (4,) + dressed.shape), "x")
    next_far = lax.ppermute(dressed_next, "x", FAR)
    next_below = lax.ppermute(dressed_next, "x", UP)
    tau = assemble(tau, above, far, below)
    tau_other = lax.ppermute(tau, "k", SWAP)
    next_above = lax.ppermute(dressed_next, "x", DOWN)
    taus = (tau, tau_other)
    parts = ladder((slabs,), taus)
    parts = ladder((dressed_next, next_below), taus, parts)
    parts = ladder((next_far, next_above), taus, parts, doubles)
    parts = exchange(parts, ("k",) + AUX)
    total = jnp.sum(parts, axis=0)
    residual = total[:, :NWIN] / denominator[:, :NWIN]
    return (total[:, NWIN : 2 * NWIN] + residual)[:, None, :]


def solution(mesh):
    fine = Mesh(mesh.devices.reshape(4, 2, 4, 2, 4, 2), PAIR + AUX)
    placed = (
        P(PAIR, AUX, None),
        P(),
        P(AUX + PAIR, None, None),
        P(AUX + PAIR, None, None),
        P(),
        P(),
        P(PAIR, None),
    )
    return jax.shard_map(
        body, mesh=fine, in_specs=placed, out_specs=P(PAIR, AUX, None), check_vma=False
    )
```

```python
import functools

import jax
import jax.numpy as jnp
from jax import lax
from jax.experimental import pallas as pl
from jax.experimental.pallas import tpu as pltpu
from jax.sharding import Mesh, PartitionSpec as P


NWIN = 8
GROUP = 256
PAIR = ("zm", "zb", "x", "k")
AUX = ("y", "zh")
SWAP = [(0, 1), (1, 0)]
UP = [(i, (i + 1) % 4) for i in range(4)]
DOWN = [(i, (i + 3) % 4) for i in range(4)]
FAR = [(i, (i + 2) % 4) for i in range(4)]
SMEM = pl.BlockSpec(memory_space=pltpu.SMEM)
VMEM = pl.BlockSpec(memory_space=pltpu.VMEM)


def start_kernel(
    pairs_ref, occ_energy_ref, vir_energy_ref, doubles_ref, singles_ref, vir_ref, occ_ref,
    dressed_ref, own_ref, denominator_ref, cols_ref,
):
    local_pairs, chunk, _ = doubles_ref.shape
    aux = lax.axis_index("y") * 2 + lax.axis_index("zh")
    singles = singles_ref[...]
    occ = singles.shape[0]
    window = singles[:, :128].astype(jnp.float32).T[:NWIN].astype(jnp.bfloat16)
    for slab in range(occ_ref.shape[0]):
        dressed = vir_ref[slab].astype(jnp.float32) - jnp.dot(
            window, occ_ref[slab], preferred_element_type=jnp.float32
        )
        dressed = dressed.astype(jnp.bfloat16)
        for copy in range(dressed_ref.shape[0]):
            dressed_ref[copy, slab * NWIN : (slab + 1) * NWIN, :] = dressed
    ids = lax.broadcasted_iota(jnp.int32, (occ, 128), 0)
    lane = lax.broadcasted_iota(jnp.int32, (occ, 128), 1)
    first = jnp.zeros((occ, 128), jnp.float32)
    for pair in range(local_pairs):
        first = jnp.where((lane == pair) & (ids == pairs_ref[pair, 0]), 1.0, first)
    cols_ref[...] = lax.dot_general(
        singles, first.astype(jnp.bfloat16), (((0,), (0,)), ((), ())), preferred_element_type=jnp.float32
    )
    cols = cols_ref[pl.ds(pl.multiple_of(aux * chunk, chunk), chunk), :]
    ids = lax.broadcasted_iota(jnp.int32, (16, occ), 1)
    row = lax.broadcasted_iota(jnp.int32, (16, occ), 0)
    second = jnp.zeros((16, occ), jnp.float32)
    for pair in range(local_pairs):
        second = jnp.where((row == pair) & (ids == pairs_ref[pair, 1]), 1.0, second)
    rows = jnp.dot(second.astype(jnp.bfloat16), singles, preferred_element_type=jnp.float32)
    for pair in range(local_pairs):
        outer = cols[:, pair : pair + 1] * rows[pair : pair + 1, :]
        tau = (doubles_ref[pair].astype(jnp.float32) + outer).astype(jnp.bfloat16)
        own_ref[pair] = tau
    lane = lax.broadcasted_iota(jnp.int32, (1, 128), 1)
    vir = jnp.zeros((1, 128), jnp.float32)
    for b in range(NWIN):
        vir = jnp.where(lane == b, vir_energy_ref[b], vir)
    for pair in range(local_pairs):
        energy = occ_energy_ref[pairs_ref[pair, 0]] + occ_energy_ref[pairs_ref[pair, 1]]
        value = (energy - vir_energy_ref[aux]) - vir
        denominator_ref[pair : pair + 1] = jnp.where(lane < NWIN, value, 0.0)


def start(doubles, singles, vir_slabs, occ_slabs, occ_energy, vir_energy, pair_list):
    local_pairs, chunk, virt = doubles.shape
    slabs, occ, _ = occ_slabs.shape
    return pl.pallas_call(
        start_kernel,
        out_shape=(
            jax.ShapeDtypeStruct((4, slabs * NWIN, virt), jnp.bfloat16),
            jax.ShapeDtypeStruct((local_pairs, chunk, virt), jnp.bfloat16),
            jax.ShapeDtypeStruct((local_pairs, 128), jnp.float32),
        ),
        in_specs=[SMEM] * 3 + [VMEM] * 4,
        out_specs=(VMEM,) * 3,
        scratch_shapes=[pltpu.VMEM((virt, 128), jnp.float32)],
        cost_estimate=pl.CostEstimate(flops=slabs * NWIN * occ * virt * 2, bytes_accessed=3 << 20, transcendentals=0),
        name="start",
    )(pair_list, occ_energy, vir_energy, doubles, singles, vir_slabs, occ_slabs)


def fold(gram):
    row = lax.broadcasted_iota(jnp.int32, (GROUP, GROUP), 0) // NWIN
    col = lax.broadcasted_iota(jnp.int32, (GROUP, GROUP), 1) // NWIN
    kept = jnp.where(row == col, gram, 0.0)
    folded = jnp.sum(kept.reshape(GROUP // NWIN, NWIN, GROUP), axis=0)
    folded = folded[:, :128] + folded[:, 128:]
    shift = 64
    while shift >= NWIN:
        folded = folded + pltpu.roll(folded, shift, 1)
        shift //= 2
    return folded


def add_rows(slabs, tau_refs, gram_ref, opens):
    for owner, tau_ref in enumerate(tau_refs):
        pairs, virt = tau_ref.shape[2], tau_ref.shape[4]
        for pair in range(pairs):
            tau = tau_ref[:, :, pair].reshape(virt, virt)
            half = jnp.dot(slabs, tau, preferred_element_type=jnp.float32).astype(jnp.bfloat16)
            gram = None if opens else gram_ref[owner * pairs + pair]
            for at in range(0, slabs.shape[0], GROUP):
                block = lax.dot_general(
                    half[at : at + GROUP],
                    slabs[at : at + GROUP],
                    (((1,), (1,)), ((), ())),
                    preferred_element_type=jnp.float32,
                )
                gram = block if gram is None else gram + block
            gram_ref[owner * pairs + pair] = gram


def ladder_kernel(near_count, far_count, has_earlier, pays, *refs):
    near_refs, refs = refs[:near_count], refs[near_count:]
    far_refs, refs = refs[:far_count], refs[far_count:]
    tau_refs, refs = refs[:2], refs[2:]
    earlier_ref = refs[0] if has_earlier else None
    doubles_ref = refs[1] if pays else None
    refs = refs[has_earlier + pays :]
    out_ref, gram_ref = refs[0], refs[1]
    copies = [
        pltpu.make_async_copy(ref, refs[2].at[at], refs[3].at[at]) for at, ref in enumerate(far_refs)
    ]
    for copy in copies:
        copy.start()
    opens = True
    for ref in near_refs:
        slabs = ref[...].reshape(-1, ref.shape[-1])
        add_rows(slabs, tau_refs, gram_ref, opens)
        opens = False
    for at, copy in enumerate(copies):
        copy.wait()
        add_rows(refs[2][at], tau_refs, gram_ref, opens)
        opens = False
    pairs = tau_refs[0].shape[2]
    core = lax.axis_index("k")
    lane = lax.broadcasted_iota(jnp.int32, (NWIN, 128), 1)
    holds = (lax.axis_index("y") == 0) & (lax.axis_index("zh") == 0)
    for owner in range(2):
        for pair in range(pairs):
            residual = fold(gram_ref[owner * pairs + pair])
            if has_earlier:
                residual = residual + earlier_ref[owner * pairs + pair]
            if not pays:
                out_ref[owner * pairs + pair] = residual
                continue
            row = jnp.where(lane < NWIN, residual, 0.0)
            if owner == 0:
                doubles = pltpu.roll(doubles_ref[pair].astype(jnp.float32)[:NWIN], NWIN, 1)
                doubles = jnp.where((lane < 2 * NWIN) & holds, doubles, 0.0)
                row = jnp.where(lane < NWIN, residual, doubles)
            to = core if owner == 0 else 1 - core
            for a in range(NWIN):
                out_ref[to * NWIN + a, pair : pair + 1, :] = row[a : a + 1]


def ladder(near, far, taus, earlier=None, doubles=None):
    pairs, virt = taus[0].shape[2], taus[0].shape[4]
    rows = sum(slab.size // virt for slab in (*near, *far))
    has_earlier, pays = earlier is not None, doubles is not None
    specs = [VMEM] * len(near) + [pl.BlockSpec(memory_space=pl.ANY)] * len(far) + [VMEM] * 2
    operands = [*near, *far, *taus]
    out = (2 * pairs, NWIN, 128)
    if has_earlier:
        specs.append(VMEM)
        operands.append(earlier)
    if pays:
        specs.append(pl.BlockSpec((pairs, 16, 128), lambda i: (0, 0, 0)))
        operands.append(doubles)
        out = (2 * NWIN, pairs, 128)
    scratch = [pltpu.VMEM((2 * pairs, GROUP, GROUP), jnp.float32)]
    if far:
        scratch.append(pltpu.VMEM((len(far),) + far[0].shape, far[0].dtype))
        scratch.append(pltpu.SemaphoreType.DMA((len(far),)))
    return pl.pallas_call(
        functools.partial(ladder_kernel, len(near), len(far), has_earlier, pays),
        out_shape=jax.ShapeDtypeStruct(out, jnp.float32),
        grid=(1,),
        in_specs=specs,
        out_specs=VMEM,
        scratch_shapes=scratch,
        cost_estimate=pl.CostEstimate(
            flops=2 * pairs * rows * virt * (virt + GROUP) * 2,
            bytes_accessed=2 * rows * virt + 4 * pairs * virt * virt,
            transcendentals=0,
        ),
        compiler_params=pltpu.CompilerParams(vmem_limit_bytes=24 << 20),
        name="ladder",
    )(*operands)


def join_kernel(own_ref, other_ref, out_ref):
    zh = lax.axis_index("zh")
    out_ref[zh] = own_ref[...]
    out_ref[1 - zh] = other_ref[...]


def join(own, other):
    return pl.pallas_call(
        join_kernel,
        out_shape=jax.ShapeDtypeStruct((2,) + own.shape, own.dtype),
        in_specs=[VMEM, VMEM],
        out_specs=VMEM,
        compiler_params=pltpu.CompilerParams(vmem_limit_bytes=4 << 20),
        name="join",
    )(own, other)


def assemble_kernel(own_ref, above_ref, far_ref, below_ref, out_ref):
    y = lax.axis_index("y")
    for step, ref in enumerate((own_ref, above_ref, far_ref, below_ref)):
        out_ref[lax.rem(y + step, 4)] = ref[...]


def assemble(own, above, far, below):
    return pl.pallas_call(
        assemble_kernel,
        out_shape=jax.ShapeDtypeStruct((4,) + own.shape, own.dtype),
        in_specs=[VMEM] * 4,
        out_specs=VMEM,
        compiler_params=pltpu.CompilerParams(vmem_limit_bytes=6 << 20),
        name="assemble",
    )(own, above, far, below)


def exchange(copies, axis):
    return lax.all_to_all(copies, axis, split_axis=0, concat_axis=0, tiled=True)


def body(doubles, singles, vir_slabs, occ_slabs, occ_energy, vir_energy, pair_list):
    virt = doubles.shape[2]
    copies, own, denominator = start(
        doubles, singles, vir_slabs, occ_slabs, occ_energy, vir_energy, pair_list
    )
    dressed = exchange(copies, "zm").reshape(-1, virt)
    other = lax.ppermute(own, "zh", SWAP)
    dressed_next = lax.ppermute(dressed, "zb", SWAP)
    tau = join(own, other)
    below = lax.ppermute(tau, "y", UP)
    above = lax.ppermute(tau, "y", DOWN)
    far = lax.ppermute(below, "y", UP)
    slabs = exchange(jnp.broadcast_to(dressed[None], (4,) + dressed.shape), "x")
    next_far = lax.ppermute(dressed_next, "x", FAR)
    next_below = lax.ppermute(dressed_next, "x", UP)
    tau = assemble(tau, above, far, below)
    tau_other = lax.ppermute(tau, "k", SWAP)
    next_above = lax.ppermute(dressed_next, "x", DOWN)
    taus = (tau, tau_other)
    parts = ladder((slabs,), (), taus)
    parts = ladder((dressed_next,), (next_far, next_below), taus, parts)
    parts = ladder((next_above,), (), taus, parts, doubles)
    parts = exchange(parts, ("k",) + AUX)
    total = jnp.sum(parts, axis=0)
    residual = total[:, :NWIN] / denominator[:, :NWIN]
    return (total[:, NWIN : 2 * NWIN] + residual)[:, None, :]


def solution(mesh):
    fine = Mesh(mesh.devices.reshape(4, 2, 4, 2, 4, 2), PAIR + AUX)
    placed = (
        P(PAIR, AUX, None),
        P(),
        P(AUX + PAIR, None, None),
        P(AUX + PAIR, None, None),
        P(),
        P(),
        P(PAIR, None),
    )
    return jax.shard_map(
        body, mesh=fine, in_specs=placed, out_specs=P(PAIR, AUX, None), check_vma=False
    )
```

```python
import functools

import jax
import jax.numpy as jnp
from jax import lax
from jax.experimental import pallas as pl
from jax.experimental.pallas import tpu as pltpu
from jax.sharding import Mesh, PartitionSpec as P


NWIN = 8
GROUP = 256
PAIR = ("zm", "zb", "x", "k")
AUX = ("y", "zh")
SWAP = [(0, 1), (1, 0)]
UP = [(i, (i + 1) % 4) for i in range(4)]
DOWN = [(i, (i + 3) % 4) for i in range(4)]
FAR = [(i, (i + 2) % 4) for i in range(4)]
SMEM = pl.BlockSpec(memory_space=pltpu.SMEM)
VMEM = pl.BlockSpec(memory_space=pltpu.VMEM)


def start_kernel(
    pairs_ref, occ_energy_ref, vir_energy_ref, doubles_ref, singles_ref, vir_ref, occ_ref,
    dressed_ref, own_ref, denominator_ref, cols_ref,
):
    local_pairs, chunk, _ = doubles_ref.shape
    aux = lax.axis_index("y") * 2 + lax.axis_index("zh")
    singles = singles_ref[...]
    occ = singles.shape[0]
    window = singles[:, :128].astype(jnp.float32).T[:NWIN].astype(jnp.bfloat16)
    for slab in range(occ_ref.shape[0]):
        dressed = vir_ref[slab].astype(jnp.float32) - jnp.dot(
            window, occ_ref[slab], preferred_element_type=jnp.float32
        )
        dressed = dressed.astype(jnp.bfloat16)
        for copy in range(dressed_ref.shape[0]):
            dressed_ref[copy, slab * NWIN : (slab + 1) * NWIN, :] = dressed
    ids = lax.broadcasted_iota(jnp.int32, (occ, 128), 0)
    lane = lax.broadcasted_iota(jnp.int32, (occ, 128), 1)
    first = jnp.zeros((occ, 128), jnp.float32)
    for pair in range(local_pairs):
        first = jnp.where((lane == pair) & (ids == pairs_ref[pair, 0]), 1.0, first)
    cols_ref[...] = lax.dot_general(
        singles, first.astype(jnp.bfloat16), (((0,), (0,)), ((), ())), preferred_element_type=jnp.float32
    )
    cols = cols_ref[pl.ds(pl.multiple_of(aux * chunk, chunk), chunk), :]
    ids = lax.broadcasted_iota(jnp.int32, (16, occ), 1)
    row = lax.broadcasted_iota(jnp.int32, (16, occ), 0)
    second = jnp.zeros((16, occ), jnp.float32)
    for pair in range(local_pairs):
        second = jnp.where((row == pair) & (ids == pairs_ref[pair, 1]), 1.0, second)
    rows = jnp.dot(second.astype(jnp.bfloat16), singles, preferred_element_type=jnp.float32)
    for pair in range(local_pairs):
        outer = cols[:, pair : pair + 1] * rows[pair : pair + 1, :]
        tau = (doubles_ref[pair].astype(jnp.float32) + outer).astype(jnp.bfloat16)
        own_ref[pair] = tau
    lane = lax.broadcasted_iota(jnp.int32, (1, 128), 1)
    vir = jnp.zeros((1, 128), jnp.float32)
    for b in range(NWIN):
        vir = jnp.where(lane == b, vir_energy_ref[b], vir)
    for pair in range(local_pairs):
        energy = occ_energy_ref[pairs_ref[pair, 0]] + occ_energy_ref[pairs_ref[pair, 1]]
        value = (energy - vir_energy_ref[aux]) - vir
        denominator_ref[pair : pair + 1] = jnp.where(lane < NWIN, value, 0.0)


def start(doubles, singles, vir_slabs, occ_slabs, occ_energy, vir_energy, pair_list):
    local_pairs, chunk, virt = doubles.shape
    slabs, occ, _ = occ_slabs.shape
    return pl.pallas_call(
        start_kernel,
        out_shape=(
            jax.ShapeDtypeStruct((4, slabs * NWIN, virt), jnp.bfloat16),
            jax.ShapeDtypeStruct((local_pairs, chunk, virt), jnp.bfloat16),
            jax.ShapeDtypeStruct((local_pairs, 128), jnp.float32),
        ),
        in_specs=[SMEM] * 3 + [VMEM] * 4,
        out_specs=(VMEM,) * 3,
        scratch_shapes=[pltpu.VMEM((virt, 128), jnp.float32)],
        cost_estimate=pl.CostEstimate(flops=slabs * NWIN * occ * virt * 2, bytes_accessed=3 << 20, transcendentals=0),
        name="start",
    )(pair_list, occ_energy, vir_energy, doubles, singles, vir_slabs, occ_slabs)


def diagonal(gram_ref, index):
    place = lax.broadcasted_iota(jnp.int32, (NWIN, 128), 1) // NWIN
    total = jnp.zeros((NWIN, 128), jnp.float32)
    per_row = 128 // NWIN
    for q in range(GROUP // NWIN):
        lanes = q // per_row * 128
        block = gram_ref[index, q * NWIN : (q + 1) * NWIN, lanes : lanes + 128]
        total = total + jnp.where(place == q % per_row, block, 0.0)
    return total


def fold(blocks):
    shift = 64
    while shift >= NWIN:
        blocks = blocks + pltpu.roll(blocks, shift, 1)
        shift //= 2
    return blocks


def add_rows(slabs, tau_refs, gram_ref, opens):
    for owner, tau_ref in enumerate(tau_refs):
        pairs, virt = tau_ref.shape[2], tau_ref.shape[4]
        for pair in range(pairs):
            tau = tau_ref[:, :, pair].reshape(virt, virt)
            half = jnp.dot(slabs, tau, preferred_element_type=jnp.float32).astype(jnp.bfloat16)
            gram = None if opens else gram_ref[owner * pairs + pair]
            for at in range(0, slabs.shape[0], GROUP):
                block = lax.dot_general(
                    half[at : at + GROUP],
                    slabs[at : at + GROUP],
                    (((1,), (1,)), ((), ())),
                    preferred_element_type=jnp.float32,
                )
                gram = block if gram is None else gram + block
            gram_ref[owner * pairs + pair] = gram


def ladder_kernel(near_count, far_count, has_earlier, pays, *refs):
    near_refs, refs = refs[:near_count], refs[near_count:]
    far_refs, refs = refs[:far_count], refs[far_count:]
    tau_refs, refs = refs[:2], refs[2:]
    earlier_ref = refs[0] if has_earlier else None
    doubles_ref = refs[1] if pays else None
    refs = refs[has_earlier + pays :]
    out_ref, gram_ref = refs[0], refs[1]
    copies = [
        pltpu.make_async_copy(ref, refs[2].at[at], refs[3].at[at]) for at, ref in enumerate(far_refs)
    ]
    for copy in copies:
        copy.start()
    opens = True
    for ref in near_refs:
        slabs = ref[...].reshape(-1, ref.shape[-1])
        add_rows(slabs, tau_refs, gram_ref, opens)
        opens = False
    for at, copy in enumerate(copies):
        copy.wait()
        add_rows(refs[2][at], tau_refs, gram_ref, opens)
        opens = False
    pairs = tau_refs[0].shape[2]
    core = lax.axis_index("k")
    lane = lax.broadcasted_iota(jnp.int32, (NWIN, 128), 1)
    holds = (lax.axis_index("y") == 0) & (lax.axis_index("zh") == 0)
    for owner in range(2):
        for pair in range(pairs):
            residual = diagonal(gram_ref, owner * pairs + pair)
            if has_earlier:
                residual = residual + earlier_ref[owner * pairs + pair]
            if not pays:
                out_ref[owner * pairs + pair] = residual
                continue
            residual = fold(residual)
            row = jnp.where(lane < NWIN, residual, 0.0)
            if owner == 0:
                doubles = pltpu.roll(doubles_ref[pair].astype(jnp.float32)[:NWIN], NWIN, 1)
                doubles = jnp.where((lane < 2 * NWIN) & holds, doubles, 0.0)
                row = jnp.where(lane < NWIN, residual, doubles)
            to = core if owner == 0 else 1 - core
            for a in range(NWIN):
                out_ref[to * NWIN + a, pair : pair + 1, :] = row[a : a + 1]


def ladder(near, far, taus, earlier=None, doubles=None):
    pairs, virt = taus[0].shape[2], taus[0].shape[4]
    rows = sum(slab.size // virt for slab in (*near, *far))
    has_earlier, pays = earlier is not None, doubles is not None
    specs = [VMEM] * len(near) + [pl.BlockSpec(memory_space=pl.ANY)] * len(far) + [VMEM] * 2
    operands = [*near, *far, *taus]
    out = (2 * pairs, NWIN, 128)
    if has_earlier:
        specs.append(VMEM)
        operands.append(earlier)
    if pays:
        specs.append(pl.BlockSpec((pairs, 16, 128), lambda i: (0, 0, 0)))
        operands.append(doubles)
        out = (2 * NWIN, pairs, 128)
    scratch = [pltpu.VMEM((2 * pairs, GROUP, GROUP), jnp.float32)]
    if far:
        scratch.append(pltpu.VMEM((len(far),) + far[0].shape, far[0].dtype))
        scratch.append(pltpu.SemaphoreType.DMA((len(far),)))
    return pl.pallas_call(
        functools.partial(ladder_kernel, len(near), len(far), has_earlier, pays),
        out_shape=jax.ShapeDtypeStruct(out, jnp.float32),
        grid=(1,),
        in_specs=specs,
        out_specs=VMEM,
        scratch_shapes=scratch,
        cost_estimate=pl.CostEstimate(
            flops=2 * pairs * rows * virt * (virt + GROUP) * 2,
            bytes_accessed=2 * rows * virt + 4 * pairs * virt * virt,
            transcendentals=0,
        ),
        compiler_params=pltpu.CompilerParams(vmem_limit_bytes=24 << 20),
        name="ladder",
    )(*operands)


def join_kernel(own_ref, other_ref, out_ref):
    zh = lax.axis_index("zh")
    out_ref[zh] = own_ref[...]
    out_ref[1 - zh] = other_ref[...]


def join(own, other):
    return pl.pallas_call(
        join_kernel,
        out_shape=jax.ShapeDtypeStruct((2,) + own.shape, own.dtype),
        in_specs=[VMEM, VMEM],
        out_specs=VMEM,
        compiler_params=pltpu.CompilerParams(vmem_limit_bytes=4 << 20),
        name="join",
    )(own, other)


def assemble_kernel(own_ref, above_ref, far_ref, below_ref, out_ref):
    y = lax.axis_index("y")
    for step, ref in enumerate((own_ref, above_ref, far_ref, below_ref)):
        out_ref[lax.rem(y + step, 4)] = ref[...]


def assemble(own, above, far, below):
    return pl.pallas_call(
        assemble_kernel,
        out_shape=jax.ShapeDtypeStruct((4,) + own.shape, own.dtype),
        in_specs=[VMEM] * 4,
        out_specs=VMEM,
        compiler_params=pltpu.CompilerParams(vmem_limit_bytes=6 << 20),
        name="assemble",
    )(own, above, far, below)


def exchange(copies, axis):
    return lax.all_to_all(copies, axis, split_axis=0, concat_axis=0, tiled=True)


def body(doubles, singles, vir_slabs, occ_slabs, occ_energy, vir_energy, pair_list):
    virt = doubles.shape[2]
    copies, own, denominator = start(
        doubles, singles, vir_slabs, occ_slabs, occ_energy, vir_energy, pair_list
    )
    dressed = exchange(copies, "zm").reshape(-1, virt)
    other = lax.ppermute(own, "zh", SWAP)
    dressed_next = lax.ppermute(dressed, "zb", SWAP)
    tau = join(own, other)
    below = lax.ppermute(tau, "y", UP)
    above = lax.ppermute(tau, "y", DOWN)
    far = lax.ppermute(below, "y", UP)
    slabs = exchange(jnp.broadcast_to(dressed[None], (4,) + dressed.shape), "x")
    next_far = lax.ppermute(dressed_next, "x", FAR)
    next_below = lax.ppermute(dressed_next, "x", UP)
    tau = assemble(tau, above, far, below)
    tau_other = lax.ppermute(tau, "k", SWAP)
    next_above = lax.ppermute(dressed_next, "x", DOWN)
    taus = (tau, tau_other)
    parts = ladder((slabs,), (), taus)
    parts = ladder((dressed_next,), (next_below, next_above), taus, parts)
    parts = ladder((next_far,), (), taus, parts, doubles)
    parts = exchange(parts, ("k",) + AUX)
    total = jnp.sum(parts, axis=0)
    residual = total[:, :NWIN] / denominator[:, :NWIN]
    return (total[:, NWIN : 2 * NWIN] + residual)[:, None, :]


def solution(mesh):
    fine = Mesh(mesh.devices.reshape(4, 2, 4, 2, 4, 2), PAIR + AUX)
    placed = (
        P(PAIR, AUX, None),
        P(),
        P(AUX + PAIR, None, None),
        P(AUX + PAIR, None, None),
        P(),
        P(),
        P(PAIR, None),
    )
    return jax.shard_map(
        body, mesh=fine, in_specs=placed, out_specs=P(PAIR, AUX, None), check_vma=False
    )
```
